32 devices in a mesh: band: 8 (over y, x, core), lev: 4 (over z).
Axes of the slice: x: 2, y: 2, z: 4, core: 2. Of those that a mesh axis runs over, the one named last changes fastest.
Arguments:
- spectral: bfloat16 [2, 2, 4, 1280, 2561], P(None, None, 'lev', 'band'), may hold values from -0.005859375 to 0.005859375
- legendre: bfloat16 [1280, 8, 2561], P('band'), may hold values from -6 to 6
- cycle_len: int32 [8], replicated, may hold values from 20 to 10256, as said below
- pair_wave: int32 [1280], replicated, may hold values from 0 to 1279, each once
- quad_weight: float32 [8], replicated, may hold values from 2 to 20
- forcing: bfloat16 [2, 4, 8, 10256], P(None, None, 'band', 'lev'), may hold values from -6 to 6
- mixing: bfloat16 [2, 4, 4], replicated, may hold values from -3 to 3
Outputs:
- tendency: bfloat16 [2, 2, 4, 1280, 2561], P(None, None, 'lev', 'band')
The draws below stay inside these ranges and needn't reach their ends.
Inputs may be any that keep to these rules, and one draw needn't show every extreme that they name: `cycle_len`: each length is 20 + 4 i for distinct cycle numbers i from 0 to 2559; the cycle of length 10256 is present in every draw. `pair_wave`: each number from 0 to 1279 appears once.
All inputs are finite; a program needn't handle non-finite values.
Results may differ from the reference program's by a relative error of at most 0.008.
Values may be sent and summed in bfloat16 or wider, within the bound.
A program may use at most 128 MiB of HBM per device.

```python
import math
import jax
import jax.numpy as jnp
from jax import lax

TRUNC = 2559
FIELDS = 2
PAIRS = 1280
PACK = 2561
CYCLES = 8
LEVELS = 4
SPAN = 2564
POINTS = 10256
N_BAND = 8
N_LEV = 4


def draw_cycle_len(key, part):
    order = jax.random.permutation(key, TRUNC).astype(jnp.int32)
    chosen = jnp.concatenate([order[:CYCLES - 1], jnp.full((1,), TRUNC, jnp.int32)])
    spots = jax.random.permutation(jax.random.fold_in(key, 7), CYCLES)
    chosen = chosen[spots]
    return (20 + 4 * chosen).astype(jnp.int32)


def level_of(stream_key, shape, shards, smallest, largest):
    def one(axis_at, shards_of):
        heights = jax.random.uniform(jax.random.fold_in(jax.random.fold_in(stream_key, 6), axis_at), (shards_of,), jnp.float32, smallest / len(shards), largest / len(shards))
        return jnp.repeat(jnp.exp(heights), shape[axis_at] // shards_of).reshape((-1,) + (1,) * (len(shape) - axis_at - 1))

    level = one(*shards[0])
    for cut in shards[1:]:
        level = level * one(*cut)
    return level


def bell_draw(own_key, dims, width, bound, pieces=(), held_as=jnp.bfloat16):
    loudness = level_of(own_key, dims, pieces, -0.22, 0.18) if pieces else 1.0
    array = jax.random.normal(own_key, dims, jnp.float32) * width * loudness
    return jnp.minimum(jnp.maximum(array, -bound), bound).astype(held_as)


def setup_inputs(seed: int = 0) -> dict:
    splits = jax.random.split(jax.random.key(seed), 8)
    spectral = bell_draw(splits[0], (2, FIELDS, LEVELS, PAIRS, PACK), (1.0 / (TRUNC + 1)), 0.005859375, ((2, 4), (3, 8)))
    legendre = bell_draw(splits[1], (PAIRS, CYCLES, PACK), 1.0, 6.0, ((0, 8),))
    cycle_len = draw_cycle_len(jax.random.fold_in(splits[7], 71), 0)
    pair_wave = jax.random.permutation(splits[3], PAIRS).astype(jnp.int32)
    quad_weight = jnp.clip(jnp.exp(jax.random.uniform(splits[4], (CYCLES,), jnp.float32, math.log(2.0), math.log(20.0))), 2.0, 20.0)
    forcing = bell_draw(splits[5], (FIELDS, LEVELS, CYCLES, POINTS), 1.0, 6.0, ((2, 8), (3, 4)))
    mixing = bell_draw(splits[6], (FIELDS, LEVELS, LEVELS), LEVELS ** -0.5, 3.0)
    return {"spectral": spectral, "legendre": legendre, "cycle_len": cycle_len, "pair_wave": pair_wave, "quad_weight": quad_weight, "forcing": forcing, "mixing": mixing}


TWO_PI = 6.283185307179586


def phases(numerator, length_value):
    residue = numerator % length_value
    angles = residue.astype(jnp.float32) * (TWO_PI / length_value.astype(jnp.float32))
    return jnp.cos(angles), jnp.sin(angles)


def lower_mask(lower_wave_list):
    column = jnp.arange(PACK, dtype=jnp.int32)
    return column[None, :] < (TRUNC + 1 - lower_wave_list)[:, None]


def reference(spectral, legendre, cycle_len, pair_wave, quad_weight, forcing, mixing):
    group_size = PAIRS // N_BAND
    spec_blocks = jnp.moveaxis(spectral.reshape(2, FIELDS, LEVELS, N_BAND, group_size, PACK), 3, 0)
    leg_blocks = legendre.reshape(N_BAND, group_size, CYCLES, PACK)
    low_blocks = pair_wave.reshape(N_BAND, group_size)

    def inverse_block(block_items):
        spec_blk, leg_blk, low_blk = block_items
        lower_part = lower_mask(low_blk)
        halves = jnp.stack([lower_part, jnp.logical_not(lower_part)], axis=1)
        masked = jnp.where(halves, spec_blk[:, :, :, :, None, :], jnp.zeros((), jnp.bfloat16))
        return jnp.einsum('rflphc,pjc->fljrph', masked.astype(jnp.float32), leg_blk.astype(jnp.float32))

    fourier = lax.map(inverse_block, (spec_blocks, leg_blocks, low_blocks))
    fourier = jnp.moveaxis(fourier, 0, 4).reshape(FIELDS, LEVELS, CYCLES, 2, TRUNC + 1)
    wave_list = jnp.stack([pair_wave, TRUNC - pair_wave], axis=1).reshape(-1)
    live_mask = 2 * wave_list[None, :] < cycle_len[:, None]
    fourier = jnp.where(live_mask[None, None, :, None, :], fourier, 0.0).astype(jnp.bfloat16)

    gauss_weight = jnp.where(wave_list == 0, 1.0, 2.0).astype(jnp.float32)
    points = jnp.arange(N_LEV, dtype=jnp.int32)[:, None] * SPAN + jnp.arange(SPAN, dtype=jnp.int32)[None, :]

    def cycle_tables(length_value):
        outer_num = wave_list[None, :] * (jnp.arange(N_LEV, dtype=jnp.int32) * SPAN)[:, None]
        outer_cos, outer_sin = phases(outer_num, length_value)
        inner_num = wave_list[:, None] * jnp.arange(SPAN, dtype=jnp.int32)[None, :]
        inner_cos, inner_sin = phases(inner_num, length_value)
        inner_table = jnp.concatenate([inner_cos, inner_sin], axis=0).astype(jnp.bfloat16)
        return outer_cos, outer_sin, inner_table

    def synthesize(block_items):
        coeffs, length_value = block_items
        outer_cos, outer_sin, inner_table = cycle_tables(length_value)
        part_re = coeffs[:, :, 0, None, :].astype(jnp.float32)
        part_im = coeffs[:, :, 1, None, :].astype(jnp.float32)
        twist_re = (gauss_weight * (part_re * outer_cos - part_im * outer_sin)).astype(jnp.bfloat16)
        twist_im = (gauss_weight * (part_re * outer_sin + part_im * outer_cos)).astype(jnp.bfloat16)
        stacked = jnp.concatenate([twist_re, -twist_im], axis=-1)
        grid_vals = jnp.einsum('flak,kb->flab', stacked.astype(jnp.float32), inner_table.astype(jnp.float32))
        return jnp.where((points < length_value)[None, None], grid_vals, 0.0)

    grid_vals = lax.map(synthesize, (jnp.moveaxis(fourier, 2, 0), cycle_len))
    grid_vals = jnp.moveaxis(grid_vals, 0, 2).reshape(FIELDS, LEVELS, CYCLES, POINTS)

    level_product = (grid_vals[0] * grid_vals[1]).astype(jnp.bfloat16)
    mixing_tendency = jnp.einsum('flm,mrp->flrp', mixing.astype(jnp.float32), level_product.astype(jnp.float32))
    summed = grid_vals + forcing.astype(jnp.float32) + mixing_tendency
    flat_points = jnp.arange(POINTS, dtype=jnp.int32)
    summed = jnp.where((flat_points[None, :] < cycle_len[:, None])[None, None], summed, 0.0)
    cycle_q = summed.astype(jnp.bfloat16)

    def analyse(block_items):
        values, length_value, cycle_weight = block_items
        outer_cos, outer_sin, inner_table = cycle_tables(length_value)
        blocks = values.reshape(FIELDS, LEVELS, N_LEV, SPAN).astype(jnp.float32)
        analysed = jnp.einsum('flab,kb->flak', blocks, inner_table.astype(jnp.float32))
        cos_part = analysed[..., :TRUNC + 1]
        sin_part = analysed[..., TRUNC + 1:]
        factor = cycle_weight / length_value.astype(jnp.float32)
        coeff_re = jnp.sum(cos_part * outer_cos - sin_part * outer_sin, axis=2) * factor
        coeff_im = -jnp.sum(cos_part * outer_sin + sin_part * outer_cos, axis=2) * factor
        keep_mask = 2 * wave_list < length_value
        coeff_re = jnp.where(keep_mask, coeff_re, 0.0)
        coeff_im = jnp.where(keep_mask, coeff_im, 0.0)
        return jnp.stack([coeff_re, coeff_im], axis=2).astype(jnp.bfloat16)

    spectral_in = lax.map(analyse, (jnp.moveaxis(cycle_q, 2, 0), cycle_len, quad_weight))
    spectral_in = spectral_in.reshape(CYCLES, FIELDS, LEVELS, 2, N_BAND, group_size, 2)
    spectral_in = jnp.moveaxis(spectral_in, 4, 0)

    def direct_block(block_items):
        coeff_blk, leg_blk, low_blk = block_items
        legendre_sum = jnp.einsum('jflrph,pjc->rflphc', coeff_blk.astype(jnp.float32), leg_blk.astype(jnp.float32))
        lower_part = lower_mask(low_blk)
        chosen = jnp.where(lower_part, legendre_sum[:, :, :, :, 0, :], legendre_sum[:, :, :, :, 1, :])
        return chosen.astype(jnp.bfloat16)

    result = lax.map(direct_block, (spectral_in, leg_blocks, low_blocks))
    return jnp.moveaxis(result, 0, 3).reshape(2, FIELDS, LEVELS, PAIRS, PACK)
```

```python
import functools

import jax
import jax.numpy as jnp
from jax import lax
from jax.experimental import pallas as pl
from jax.experimental.pallas import tpu as pltpu
from jax.sharding import PartitionSpec as P

TRUNC = 2559
FIELDS = 2
INNER = 256
CHUNK = 256
TWO_PI = 6.283185307179586


def pair_block(pair_dev):
    return 16 if pair_dev % 16 == 0 else 8


def sincos(wave, point, length, inverse_length):
    number = wave * point
    turns = jnp.floor(number.astype(jnp.float32) * inverse_length).astype(jnp.int32)
    residue = (number - turns * length).astype(jnp.float32) * inverse_length
    quarter = jnp.floor(residue * 4.0 + 0.5)
    t = (residue - quarter * 0.25) * TWO_PI
    t2 = t * t
    sin_t = t * (1.0 + t2 * (-1.0 / 6 + t2 * (1.0 / 120 + t2 * (-1.0 / 5040 + t2 * (1.0 / 362880)))))
    cos_t = 1.0 + t2 * (
        -0.5 + t2 * (1.0 / 24 + t2 * (-1.0 / 720 + t2 * (1.0 / 40320 + t2 * (-1.0 / 3628800))))
    )
    q = quarter.astype(jnp.int32)
    swap = (q & 1) == 1
    cos_v = jnp.where(swap, sin_t, cos_t)
    sin_v = jnp.where(swap, cos_t, sin_t)
    cos_v = jnp.where(((q + 1) & 2) == 2, -cos_v, cos_v)
    sin_v = jnp.where((q & 2) == 2, -sin_v, sin_v)
    return cos_v, sin_v


def diagonal(pairs, cycles):
    rows = lax.broadcasted_iota(jnp.int32, (pairs, cycles, 8 * pairs), 0)
    lanes = lax.broadcasted_iota(jnp.int32, (pairs, cycles, 8 * pairs), 2) % pairs
    return rows == lanes


def inverse_kernel(limit_ref, spec_ref, leg_ref, out_ref):
    pairs, cycles, packed = leg_ref.shape
    column = lax.broadcasted_iota(jnp.int32, (pairs, packed), 1)
    lower = column < limit_ref[...]
    lows, highs = [], []
    for s in range(2):
        for f in range(FIELDS):
            row = spec_ref[s, f, 0].astype(jnp.float32)
            lows.append(jnp.where(lower, row, 0.0))
            highs.append(jnp.where(lower, 0.0, row))
    spec = jnp.concatenate(lows + highs, axis=0).astype(jnp.bfloat16)
    leg = leg_ref[...].reshape(pairs * cycles, packed)
    full = lax.dot_general(
        leg, spec, (((1,), (1,)), ((), ())), preferred_element_type=jnp.float32
    )
    full = full.reshape(pairs, cycles, 8 * pairs)
    out_ref[0] = jnp.sum(jnp.where(diagonal(pairs, cycles), full, 0.0), axis=0)


def direct_kernel(limit_ref, coeff_ref, leg_ref, out_ref):
    pairs, cycles, packed = leg_ref.shape
    wide = jnp.broadcast_to(coeff_ref[...], (pairs, cycles, 8 * pairs))
    wide = jnp.where(diagonal(pairs, cycles), wide, 0.0).reshape(pairs * cycles, 8 * pairs)
    wide = wide.T.astype(jnp.bfloat16)
    leg = leg_ref[...].reshape(pairs * cycles, packed)
    full = jnp.dot(wide, leg, preferred_element_type=jnp.float32)
    column = lax.broadcasted_iota(jnp.int32, (pairs, packed), 1)
    lower = column < limit_ref[...]
    for s in range(2):
        for f in range(FIELDS):
            at = (s * FIELDS + f) * pairs
            low = full[at : at + pairs]
            high = full[4 * pairs + at : 4 * pairs + at + pairs]
            out_ref[s, f, 0] = jnp.where(lower, low, high).astype(jnp.bfloat16)


def grid_kernel(
    points_dev, scalars_ref, factors_ref, wave_ref, four_ref, forcing_ref, mixing_ref, out_ref,
    cos_tab, sin_tab, cos_out, sin_out, twist_re, twist_im,
):
    rows, waves = four_ref.shape[1], four_ref.shape[2]
    levels = rows // FIELDS
    outer = cos_out.shape[0]
    used = pl.cdiv(points_dev, INNER)
    length = scalars_ref[0]
    base = scalars_ref[1]
    inverse_length = factors_ref[0]
    factor = factors_ref[1]

    @pl.loop(0, waves // CHUNK)
    def _(c):
        span = pl.ds(pl.multiple_of(c * CHUNK, CHUNK), CHUNK)
        wave = wave_ref[:, span]
        eight = lax.broadcasted_iota(jnp.int32, (8, CHUNK), 0)
        c0, s0 = sincos(wave, eight, length, inverse_length)
        c1, s1 = sincos(wave, eight * 8, length, inverse_length)
        c2, s2 = sincos(wave, eight * 64, length, inverse_length)
        steps = lax.broadcasted_iota(jnp.int32, (outer, CHUNK), 0)
        c3, s3 = sincos(wave, base + steps * INNER, length, inverse_length)
        cos_out[:, span] = c3
        sin_out[:, span] = s3
        for high in range(INNER // 64):
            ch, sh = c2[high : high + 1], s2[high : high + 1]
            for mid in range(8):
                cm, sm = c1[mid : mid + 1], s1[mid : mid + 1]
                cj, sj = ch * cm - sh * sm, ch * sm + sh * cm
                at = high * 64 + mid * 8
                cos_tab[at : at + 8, span] = (c0 * cj - s0 * sj).astype(jnp.bfloat16)
                sin_tab[at : at + 8, span] = (s0 * cj + c0 * sj).astype(jnp.bfloat16)

    @pl.loop(0, waves // CHUNK)
    def _(c):
        span = pl.ds(pl.multiple_of(c * CHUNK, CHUNK), CHUNK)
        wave = wave_ref[:, span]
        gain = jnp.where(wave == 0, 1.0, 2.0)
        gain = jnp.where(2 * wave < length, gain, 0.0)
        live = gain > 0.0
        re = jnp.where(live, four_ref[0, :, span].astype(jnp.float32) * gain, 0.0)
        im = jnp.where(live, four_ref[1, :, span].astype(jnp.float32) * gain, 0.0)
        for a in range(used):
            co, so = cos_out[a : a + 1, span], sin_out[a : a + 1, span]
            twist_re[a * rows : (a + 1) * rows, span] = (re * co - im * so).astype(jnp.bfloat16)
            twist_im[a * rows : (a + 1) * rows, span] = -(re * so + im * co).astype(jnp.bfloat16)

    contract = (((1,), (1,)), ((), ()))
    grid = lax.dot_general(
        twist_re[...], cos_tab[...], contract, preferred_element_type=jnp.float32
    ) + lax.dot_general(twist_im[...], sin_tab[...], contract, preferred_element_type=jnp.float32)
    lane = lax.broadcasted_iota(jnp.int32, (rows, INNER), 1)
    updated = []
    for a in range(used):
        point = a * INNER + lane
        inside = (point < points_dev) & (base + point < length)
        cell = jnp.where(inside, grid[a * rows : (a + 1) * rows], 0.0)
        product = (cell[:levels] * cell[levels:]).astype(jnp.bfloat16).astype(jnp.float32)
        total = cell + forcing_ref[:, a * INNER : (a + 1) * INNER].astype(jnp.float32)
        for l2 in range(levels):
            total = total + mixing_ref[:, l2 : l2 + 1] * product[l2 : l2 + 1]
        updated.append(jnp.where(inside, total, 0.0))
    updated = jnp.concatenate(updated, axis=0).astype(jnp.bfloat16)

    @pl.loop(0, waves // CHUNK)
    def _(c):
        span = pl.ds(pl.multiple_of(c * CHUNK, CHUNK), CHUNK)
        cos_part = jnp.dot(updated, cos_tab[:, span], preferred_element_type=jnp.float32)
        sin_part = jnp.dot(updated, sin_tab[:, span], preferred_element_type=jnp.float32)
        re = jnp.zeros((rows, CHUNK), jnp.float32)
        im = jnp.zeros((rows, CHUNK), jnp.float32)
        for a in range(used):
            co, so = cos_out[a : a + 1, span], sin_out[a : a + 1, span]
            cp, sp = cos_part[a * rows : (a + 1) * rows], sin_part[a * rows : (a + 1) * rows]
            re = re + (cp * co - sp * so)
            im = im + (cp * so + sp * co)
        keep = 2 * wave_ref[:, span] < length
        out_ref[0, :, span] = jnp.where(keep, re * factor, 0.0).astype(jnp.bfloat16)
        out_ref[1, :, span] = jnp.where(keep, im * -factor, 0.0).astype(jnp.bfloat16)


def on_device(spectral, legendre, cycle_len, pair_wave, quad_weight, forcing, mixing):
    band_count = lax.axis_size("band")
    lev_count = lax.axis_size("lev")
    band_id = lax.axis_index("band")
    lev_id = lax.axis_index("lev")
    pair_dev, packed = spectral.shape[3], spectral.shape[4]
    cycles = legendre.shape[1]
    levels, points_dev = forcing.shape[1], forcing.shape[3]
    rows = FIELDS * levels
    waves = 2 * band_count * pair_dev
    pairs = pair_block(pair_dev)
    blocks = pair_dev // pairs

    my_low = lax.dynamic_slice_in_dim(pair_wave, band_id * pair_dev, pair_dev)
    limit = (TRUNC + 1 - my_low)[:, None]
    spec_spec = pl.BlockSpec((2, FIELDS, 1, pairs, packed), lambda i: (0, 0, 0, i, 0))
    leg_spec = pl.BlockSpec((pairs, cycles, packed), lambda i: (i, 0, 0))
    limit_spec = pl.BlockSpec((pairs, 1), lambda i: (i, 0))
    cell_spec = pl.BlockSpec((1, cycles, 8 * pairs), lambda i: (i, 0, 0))
    four = pl.pallas_call(
        inverse_kernel,
        grid=(blocks,),
        in_specs=[limit_spec, spec_spec, leg_spec],
        out_specs=cell_spec,
        out_shape=jax.ShapeDtypeStruct((blocks, cycles, 8 * pairs), jnp.float32),
    )(limit, spectral, legendre)
    four = four.astype(jnp.bfloat16).reshape(blocks, cycles, 2, 4, pairs)
    four = jnp.transpose(four, (1, 3, 0, 2, 4)).reshape(cycles, 1, 4 * blocks * 2 * pairs)
    four = jnp.broadcast_to(four, (cycles, lev_count, four.shape[2]))
    four = four.reshape(band_count * lev_count, four.shape[2])
    four = lax.all_to_all(four, ("band", "lev"), split_axis=0, concat_axis=0, tiled=True)
    four = four.reshape(band_count, lev_count, 2, FIELDS, 2 * pair_dev)
    four = jnp.transpose(four, (2, 3, 1, 0, 4)).reshape(2, rows, waves)

    low = pair_wave.reshape(band_count, blocks, 1, pairs)
    wave = jnp.concatenate([low, TRUNC - low], axis=2).reshape(1, waves)
    my_len = lax.dynamic_index_in_dim(cycle_len, band_id, 0, keepdims=False)
    my_weight = lax.dynamic_index_in_dim(quad_weight, band_id, 0, keepdims=False)
    length_f = my_len.astype(jnp.float32)
    scalars = jnp.stack([my_len, lev_id * points_dev])
    factors = jnp.stack([1.0 / length_f, my_weight / length_f])
    used = pl.cdiv(points_dev, INNER)
    outer = pl.cdiv(used, 8) * 8
    force = jnp.pad(forcing.reshape(rows, points_dev), ((0, 0), (0, used * INNER - points_dev)))
    vmem = pl.BlockSpec(memory_space=pltpu.VMEM)
    smem = pl.BlockSpec(memory_space=pltpu.SMEM)
    partial = pl.pallas_call(
        functools.partial(grid_kernel, points_dev),
        in_specs=[smem, smem, vmem, vmem, vmem, vmem],
        out_specs=vmem,
        out_shape=jax.ShapeDtypeStruct((2, rows, waves), jnp.bfloat16),
        scratch_shapes=[
            pltpu.VMEM((INNER, waves), jnp.bfloat16),
            pltpu.VMEM((INNER, waves), jnp.bfloat16),
            pltpu.VMEM((outer, waves), jnp.float32),
            pltpu.VMEM((outer, waves), jnp.float32),
            pltpu.VMEM((used * rows, waves), jnp.bfloat16),
            pltpu.VMEM((used * rows, waves), jnp.bfloat16),
        ],
    )(scalars, factors, wave, four, force, mixing.reshape(rows, levels).astype(jnp.float32))

    back = partial.reshape(2, FIELDS, lev_count, band_count, 2 * pair_dev)
    back = jnp.transpose(back, (3, 2, 0, 1, 4)).reshape(band_count * lev_count, 8 * pair_dev)
    back = lax.all_to_all(back, ("band", "lev"), split_axis=0, concat_axis=0, tiled=True)
    back = back.reshape(band_count, lev_count, 4, blocks, 2, pairs).astype(jnp.float32)
    back = jnp.sum(back, axis=1)
    coeff = jnp.transpose(back, (2, 0, 3, 1, 4)).reshape(blocks, cycles, 8 * pairs)
    return pl.pallas_call(
        direct_kernel,
        grid=(blocks,),
        in_specs=[limit_spec, cell_spec, leg_spec],
        out_specs=spec_spec,
        out_shape=jax.ShapeDtypeStruct(spectral.shape, jnp.bfloat16),
    )(limit, coeff, legendre)


def solution(mesh):
    return jax.shard_map(
        on_device,
        mesh=mesh,
        in_specs=(
            P(None, None, "lev", "band", None),
            P("band", None, None),
            P(),
            P(),
            P(),
            P(None, None, "band", "lev"),
            P(),
        ),
        out_specs=P(None, None, "lev", "band", None),
        check_vma=False,
    )
```

```python
import functools

import jax
import jax.numpy as jnp
from jax import lax
from jax.experimental import pallas as pl
from jax.experimental.pallas import tpu as pltpu
from jax.sharding import PartitionSpec as P

TRUNC = 2559
FIELDS = 2
INNER = 256
TWO_PI = 6.283185307179586


def pair_block(pair_dev):
    return 16 if pair_dev % 16 == 0 else 8


def sincos(wave, point, length, inverse_length):
    number = wave * point
    turns = jnp.floor(number.astype(jnp.float32) * inverse_length).astype(jnp.int32)
    residue = (number - turns * length).astype(jnp.float32) * inverse_length
    quarter = jnp.floor(residue * 4.0 + 0.5)
    t = (residue - quarter * 0.25) * TWO_PI
    t2 = t * t
    sin_t = t * (1.0 + t2 * (-1.0 / 6 + t2 * (1.0 / 120 + t2 * (-1.0 / 5040 + t2 * (1.0 / 362880)))))
    cos_t = 1.0 + t2 * (
        -0.5 + t2 * (1.0 / 24 + t2 * (-1.0 / 720 + t2 * (1.0 / 40320 + t2 * (-1.0 / 3628800))))
    )
    q = quarter.astype(jnp.int32)
    swap = (q & 1) == 1
    cos_v = jnp.where(swap, sin_t, cos_t)
    sin_v = jnp.where(swap, cos_t, sin_t)
    cos_v = jnp.where(((q + 1) & 2) == 2, -cos_v, cos_v)
    sin_v = jnp.where((q & 2) == 2, -sin_v, sin_v)
    return cos_v, sin_v


def diagonal(pairs, cycles):
    rows = lax.broadcasted_iota(jnp.int32, (pairs, cycles, 8 * pairs), 0)
    lanes = lax.broadcasted_iota(jnp.int32, (pairs, cycles, 8 * pairs), 2) % pairs
    return rows == lanes


def inverse_kernel(limit_ref, spec_ref, leg_ref, out_ref):
    pairs, cycles, packed = leg_ref.shape
    column = lax.broadcasted_iota(jnp.int32, (pairs, packed), 1)
    lower = column < limit_ref[...]
    halves = []
    for s in range(2):
        for f in range(FIELDS):
            row = spec_ref[s, f, 0].astype(jnp.float32)
            halves += [jnp.where(lower, row, 0.0), jnp.where(lower, 0.0, row)]
    spec = jnp.concatenate(halves, axis=0).astype(jnp.bfloat16)
    leg = leg_ref[...].reshape(pairs * cycles, packed)
    full = lax.dot_general(
        leg, spec, (((1,), (1,)), ((), ())), preferred_element_type=jnp.float32
    )
    full = full.reshape(pairs, cycles, 8 * pairs)
    out_ref[0] = jnp.sum(jnp.where(diagonal(pairs, cycles), full, 0.0), axis=0)


def direct_kernel(limit_ref, coeff_ref, leg_ref, out_ref):
    pairs, cycles, packed = leg_ref.shape
    wide = jnp.broadcast_to(coeff_ref[...], (pairs, cycles, 8 * pairs))
    wide = jnp.where(diagonal(pairs, cycles), wide, 0.0).reshape(pairs * cycles, 8 * pairs)
    wide = wide.T.astype(jnp.bfloat16)
    leg = leg_ref[...].reshape(pairs * cycles, packed)
    full = jnp.dot(wide, leg, preferred_element_type=jnp.float32)
    column = lax.broadcasted_iota(jnp.int32, (pairs, packed), 1)
    lower = column < limit_ref[...]
    for s in range(2):
        for f in range(FIELDS):
            at = (s * FIELDS + f) * 2 * pairs
            low = full[at : at + pairs]
            high = full[at + pairs : at + 2 * pairs]
            out_ref[s, f, 0] = jnp.where(lower, low, high).astype(jnp.bfloat16)


def grid_kernel(
    points_dev, levs, length_ref, weight_ref, wave_ref, four_ref, forcing_ref, mixing_ref, out_ref,
    cos_tab, sin_tab, cos_out, sin_out, twist_re, twist_im,
    outgoing, incoming, partial, arrived, send_sem, recv_sem, send_back, recv_back,
):
    blocks, cycles, wide = four_ref.shape
    each = wide // 4
    rows = FIELDS * levs
    outer = cos_out.shape[0]
    used = pl.cdiv(points_dev, INNER)
    slots, _, lanes = incoming.shape
    bands = slots // levs
    band_id = lax.axis_index("band")
    lev_id = lax.axis_index("lev")
    me = band_id * levs + lev_id
    length = length_ref[band_id]
    base = lev_id * points_dev
    inverse_length = 1.0 / jnp.full((1, lanes), length, jnp.int32).astype(jnp.float32)
    factor = inverse_length * weight_ref[band_id]

    barrier = pltpu.get_barrier_semaphore()

    def other(step):
        peer = (me + step) % slots
        return peer // levs, peer % levs

    @pl.loop(1, slots)
    def _(step):
        band, lev = other(step)
        pl.semaphore_signal(
            barrier, inc=1, device_id={"band": band, "lev": lev}, device_id_type=pl.DeviceIdType.MESH
        )

    sides = []
    for k in range(4):
        parts = [four_ref[i, :, k * each : (k + 1) * each] for i in range(blocks)]
        if lanes > blocks * each:
            parts.append(jnp.zeros((cycles, lanes - blocks * each), jnp.float32))
        sides.append(jnp.concatenate(parts, axis=1))
    for j in range(cycles):
        block = jnp.concatenate([side[j : j + 1] for side in sides], axis=0)
        outgoing[j] = block.astype(jnp.bfloat16)

    def tables(c):
        span = pl.ds(pl.multiple_of(c * lanes, lanes), lanes)
        wave = wave_ref[:, span]
        eight = lax.broadcasted_iota(jnp.int32, (8, lanes), 0)
        c0, s0 = sincos(wave, eight, length, inverse_length)
        c1, s1 = sincos(wave, eight * 8, length, inverse_length)
        c2, s2 = sincos(wave, eight * 64, length, inverse_length)
        steps = lax.broadcasted_iota(jnp.int32, (outer, lanes), 0)
        c3, s3 = sincos(wave, base + steps * INNER, length, inverse_length)
        cos_out[:, span] = c3
        sin_out[:, span] = s3
        for high in range(INNER // 64):
            ch, sh = c2[high : high + 1], s2[high : high + 1]
            for mid in range(8):
                cm, sm = c1[mid : mid + 1], s1[mid : mid + 1]
                cj, sj = ch * cm - sh * sm, ch * sm + sh * cm
                at = high * 64 + mid * 8
                cos_tab[at : at + 8, span] = (c0 * cj - s0 * sj).astype(jnp.bfloat16)
                sin_tab[at : at + 8, span] = (s0 * cj + c0 * sj).astype(jnp.bfloat16)

    early = bands // 2
    pl.loop(0, early)(tables)
    pl.semaphore_wait(barrier, slots - 1)

    @pl.loop(1, slots)
    def _(step):
        band, lev = other(step)
        pltpu.make_async_remote_copy(
            src_ref=outgoing.at[band], dst_ref=incoming.at[me], send_sem=send_sem,
            recv_sem=recv_sem, device_id={"band": band, "lev": lev},
            device_id_type=pl.DeviceIdType.MESH,
        ).start()

    incoming[me] = outgoing[band_id]
    pl.loop(early, bands)(tables)

    def wait_all(semaphore, buffer):
        most = buffer.at[pl.ds(0, slots - 1)]
        pltpu.make_async_copy(most, most, semaphore).wait()

    wait_all(recv_sem, incoming)

    @pl.loop(0, bands)
    def _(c):
        span = pl.ds(pl.multiple_of(c * lanes, lanes), lanes)
        wave = wave_ref[:, span]
        gain = jnp.where(wave == 0, 1.0, 2.0)
        live = 2 * wave < length
        cells = [incoming[c * levs + lev].astype(jnp.float32) for lev in range(levs)]
        order = [(f, lev) for f in range(FIELDS) for lev in range(levs)]
        re = jnp.concatenate([cells[lev][f : f + 1] for f, lev in order], axis=0)
        im = jnp.concatenate([cells[lev][FIELDS + f : FIELDS + f + 1] for f, lev in order], axis=0)
        re = jnp.where(live, re * gain, 0.0)
        im = jnp.where(live, im * gain, 0.0)
        for a in range(used):
            co, so = cos_out[a : a + 1, span], sin_out[a : a + 1, span]
            twist_re[a * rows : (a + 1) * rows, span] = (re * co - im * so).astype(jnp.bfloat16)
            twist_im[a * rows : (a + 1) * rows, span] = -(re * so + im * co).astype(jnp.bfloat16)

    contract = (((1,), (1,)), ((), ()))
    grid = lax.dot_general(
        twist_re[...], cos_tab[...], contract, preferred_element_type=jnp.float32
    ) + lax.dot_general(twist_im[...], sin_tab[...], contract, preferred_element_type=jnp.float32)
    lane = lax.broadcasted_iota(jnp.int32, (rows, INNER), 1)
    mixing = mixing_ref[...].astype(jnp.float32)
    updated = []
    for a in range(used):
        point = a * INNER + lane
        inside = (point < points_dev) & (base + point < length)
        cell = jnp.where(inside, grid[a * rows : (a + 1) * rows], 0.0)
        product = (cell[:levs] * cell[levs:]).astype(jnp.bfloat16).astype(jnp.float32)
        total = cell + forcing_ref[:, a * INNER : (a + 1) * INNER].astype(jnp.float32)
        for l2 in range(levs):
            total = total + mixing[:, l2 : l2 + 1] * product[l2 : l2 + 1]
        updated.append(jnp.where(inside, total, 0.0))
    updated = jnp.concatenate(updated, axis=0).astype(jnp.bfloat16)

    def send_band(band):
        @pl.loop(0, levs)
        def _(lev):
            @pl.when((band != band_id) | (lev != lev_id))
            def _():
                pltpu.make_async_remote_copy(
                    src_ref=partial.at[band * levs + lev], dst_ref=arrived.at[me],
                    send_sem=send_back, recv_sem=recv_back, device_id={"band": band, "lev": lev},
                    device_id_type=pl.DeviceIdType.MESH,
                ).start()

    @pl.loop(0, bands)
    def _(c):
        span = pl.ds(pl.multiple_of(c * lanes, lanes), lanes)
        cos_part = jnp.dot(updated, cos_tab[:, span], preferred_element_type=jnp.float32)
        sin_part = jnp.dot(updated, sin_tab[:, span], preferred_element_type=jnp.float32)
        re = jnp.zeros((rows, lanes), jnp.float32)
        im = jnp.zeros((rows, lanes), jnp.float32)
        for a in range(used):
            co, so = cos_out[a : a + 1, span], sin_out[a : a + 1, span]
            cp, sp = cos_part[a * rows : (a + 1) * rows], sin_part[a * rows : (a + 1) * rows]
            re = re + (cp * co - sp * so)
            im = im + (cp * so + sp * co)
        keep = 2 * wave_ref[:, span] < length
        re = jnp.where(keep, re * factor, 0.0)
        im = jnp.where(keep, im * -factor, 0.0)
        for lev in range(levs):
            picks = [side[f * levs + lev : f * levs + lev + 1] for side in (re, im) for f in range(FIELDS)]
            partial[c * levs + lev] = jnp.concatenate(picks, axis=0).astype(jnp.bfloat16)

        @pl.when(c > 0)
        def _():
            send_band(c - 1)

    arrived[me] = partial[me]
    send_band(bands - 1)
    wait_all(recv_back, arrived)
    sums = []
    for j in range(cycles):
        total = arrived[j * levs].astype(jnp.float32)
        for lev in range(1, levs):
            total = total + arrived[j * levs + lev].astype(jnp.float32)
        sums.append(total)
    for k in range(4):
        side = jnp.concatenate([total[k : k + 1] for total in sums], axis=0)
        for i in range(blocks):
            out_ref[i, :, k * each : (k + 1) * each] = side[:, i * each : (i + 1) * each]
    wait_all(send_sem, incoming)
    wait_all(send_back, arrived)


def on_device(spectral, legendre, cycle_len, pair_wave, quad_weight, forcing, mixing):
    band_count = lax.axis_size("band")
    lev_count = lax.axis_size("lev")
    band_id = lax.axis_index("band")
    lev_id = lax.axis_index("lev")
    pair_dev, packed = spectral.shape[3], spectral.shape[4]
    cycles = legendre.shape[1]
    levels, points_dev = forcing.shape[1], forcing.shape[3]
    rows = FIELDS * levels
    pairs = pair_block(pair_dev)
    blocks = pair_dev // pairs

    my_low = lax.dynamic_slice_in_dim(pair_wave, band_id * pair_dev, pair_dev)
    limit = (TRUNC + 1 - my_low)[:, None]
    spec_spec = pl.BlockSpec((2, FIELDS, 1, pairs, packed), lambda i: (0, 0, 0, i, 0))
    leg_spec = pl.BlockSpec((pairs, cycles, packed), lambda i: (i, 0, 0))
    limit_spec = pl.BlockSpec((pairs, 1), lambda i: (i, 0))
    cell_spec = pl.BlockSpec((1, cycles, 8 * pairs), lambda i: (i, 0, 0))
    four = pl.pallas_call(
        inverse_kernel,
        grid=(blocks,),
        in_specs=[limit_spec, spec_spec, leg_spec],
        out_specs=cell_spec,
        out_shape=jax.ShapeDtypeStruct((blocks, cycles, 8 * pairs), jnp.float32),
    )(limit, spectral, legendre)
    each_band = pl.cdiv(2 * pair_dev, 128) * 128
    low = pair_wave.reshape(band_count, blocks, 1, pairs)
    wave = jnp.concatenate([low, TRUNC - low], axis=2).reshape(band_count, 2 * pair_dev)
    dead = jnp.full((band_count, each_band - 2 * pair_dev), 1 << 14, jnp.int32)
    waves = band_count * each_band
    wave = jnp.concatenate([wave, dead], axis=1).reshape(1, waves)
    used = pl.cdiv(points_dev, INNER)
    outer = pl.cdiv(used, 8) * 8
    force = jnp.pad(forcing.reshape(rows, points_dev), ((0, 0), (0, used * INNER - points_dev)))
    vmem = pl.BlockSpec(memory_space=pltpu.VMEM)
    smem = pl.BlockSpec(memory_space=pltpu.SMEM)
    slots = band_count * lev_count
    message = pltpu.VMEM((slots, 2 * FIELDS, each_band), jnp.bfloat16)
    coeff = pl.pallas_call(
        functools.partial(grid_kernel, points_dev, lev_count),
        in_specs=[smem, smem, vmem, vmem, vmem, vmem],
        out_specs=vmem,
        out_shape=jax.ShapeDtypeStruct((blocks, cycles, 8 * pairs), jnp.float32),
        scratch_shapes=[
            pltpu.VMEM((INNER, waves), jnp.bfloat16),
            pltpu.VMEM((INNER, waves), jnp.bfloat16),
            pltpu.VMEM((outer, waves), jnp.float32),
            pltpu.VMEM((outer, waves), jnp.float32),
            pltpu.VMEM((used * rows, waves), jnp.bfloat16),
            pltpu.VMEM((used * rows, waves), jnp.bfloat16),
            pltpu.VMEM((cycles, 2 * FIELDS, each_band), jnp.bfloat16),
            message, message, message,
        ]
        + [pltpu.SemaphoreType.DMA] * 4,
        compiler_params=pltpu.CompilerParams(collective_id=0, has_side_effects=True),
    )(cycle_len, quad_weight, wave, four, force, mixing.reshape(rows, levels))
    return pl.pallas_call(
        direct_kernel,
        grid=(blocks,),
        in_specs=[limit_spec, cell_spec, leg_spec],
        out_specs=spec_spec,
        out_shape=jax.ShapeDtypeStruct(spectral.shape, jnp.bfloat16),
    )(limit, coeff, legendre)


def solution(mesh):
    return jax.shard_map(
        on_device,
        mesh=mesh,
        in_specs=(
            P(None, None, "lev", "band", None),
            P("band", None, None),
            P(),
            P(),
            P(),
            P(None, None, "band", "lev"),
            P(),
        ),
        out_specs=P(None, None, "lev", "band", None),
        check_vma=False,
    )
```

```python
import functools

import jax
import jax.numpy as jnp
from jax import lax
from jax.experimental import pallas as pl
from jax.experimental.pallas import tpu as pltpu
from jax.sharding import PartitionSpec as P

TRUNC = 2559
FIELDS = 2
INNER = 256
TWO_PI = 6.283185307179586


def pair_block(pair_dev):
    return 16 if pair_dev % 16 == 0 else 8


def sincos(wave, point, length, inverse_length):
    number = wave * point
    turns = jnp.floor(number.astype(jnp.float32) * inverse_length).astype(jnp.int32)
    residue = (number - turns * length).astype(jnp.float32) * inverse_length
    quarter = jnp.floor(residue * 4.0 + 0.5)
    t = (residue - quarter * 0.25) * TWO_PI
    t2 = t * t
    sin_t = t * (1.0 + t2 * (-1.0 / 6 + t2 * (1.0 / 120 + t2 * (-1.0 / 5040 + t2 * (1.0 / 362880)))))
    cos_t = 1.0 + t2 * (
        -0.5 + t2 * (1.0 / 24 + t2 * (-1.0 / 720 + t2 * (1.0 / 40320 + t2 * (-1.0 / 3628800))))
    )
    q = quarter.astype(jnp.int32)
    swap = (q & 1) == 1
    cos_v = jnp.where(swap, sin_t, cos_t)
    sin_v = jnp.where(swap, cos_t, sin_t)
    cos_v = jnp.where(((q + 1) & 2) == 2, -cos_v, cos_v)
    sin_v = jnp.where((q & 2) == 2, -sin_v, sin_v)
    return cos_v, sin_v


def diagonal(pairs, cycles):
    rows = lax.broadcasted_iota(jnp.int32, (pairs, cycles, 8 * pairs), 0)
    lanes = lax.broadcasted_iota(jnp.int32, (pairs, cycles, 8 * pairs), 2) % pairs
    return rows == lanes


def read_chunk(leg_hbm, leg_vmem, sem, pairs, i):
    part = pl.ds(pl.multiple_of(i * pairs, pairs), pairs)
    return pltpu.make_async_copy(leg_hbm.at[part], leg_vmem.at[part], sem.at[i])


def direct_kernel(limit_ref, coeff_ref, leg_hbm, out_hbm, leg_vmem, out_vmem, in_sem, out_sem):
    blocks, cycles, wide_lanes = coeff_ref.shape
    pairs = wide_lanes // 8
    packed = leg_vmem.shape[2]

    def write(i):
        part = pl.ds(pl.multiple_of(i * pairs, pairs), pairs)
        return pltpu.make_async_copy(
            out_vmem.at[:, :, :, part], out_hbm.at[:, :, :, part], out_sem.at[i]
        )

    for i in range(blocks):
        read_chunk(leg_hbm, leg_vmem, in_sem, pairs, i).start()
    mask = diagonal(pairs, cycles)
    column = lax.broadcasted_iota(jnp.int32, (pairs, packed), 1)

    @pl.loop(0, blocks)
    def _(i):
        part = pl.ds(pl.multiple_of(i * pairs, pairs), pairs)
        wide = jnp.broadcast_to(coeff_ref[pl.ds(i, 1)], (pairs, cycles, 8 * pairs))
        wide = jnp.where(mask, wide, 0.0).reshape(pairs * cycles, 8 * pairs)
        wide = wide.T.astype(jnp.bfloat16)
        lower = column < limit_ref[part]
        read_chunk(leg_hbm, leg_vmem, in_sem, pairs, i).wait()
        leg = leg_vmem[part].reshape(pairs * cycles, packed)
        full = jnp.dot(wide, leg, preferred_element_type=jnp.float32)
        for s in range(2):
            for f in range(FIELDS):
                at = (s * FIELDS + f) * 2 * pairs
                low = full[at : at + pairs]
                high = full[at + pairs : at + 2 * pairs]
                out_vmem[s, f, 0, part] = jnp.where(lower, low, high).astype(jnp.bfloat16)
        write(i).start()

    for i in range(blocks):
        write(i).wait()


def grid_kernel(
    points_dev, levs, length_ref, weight_ref, low_ref, forcing_ref, mixing_ref, spec_hbm, leg_hbm,
    out_ref, limit_ref,
    cos_tab, sin_tab, cos_out, sin_out, twist_re, twist_im,
    outgoing, incoming, partial, arrived, leg_vmem, spec_vmem, four_ref, wave_ref,
    send_sem, recv_sem, send_back, recv_back, leg_sem, spec_sem,
):
    blocks, cycles, wide = four_ref.shape
    pairs = wide // 8
    packed = leg_vmem.shape[2]
    each = wide // 4

    def read_spec(i):
        part = pl.ds(pl.multiple_of(i * pairs, pairs), pairs)
        return pltpu.make_async_copy(
            spec_hbm.at[:, :, :, part], spec_vmem.at[:, :, :, part], spec_sem.at[i]
        )

    for i in range(blocks):
        read_spec(i).start()
        read_chunk(leg_hbm, leg_vmem, leg_sem, pairs, i).start()
    rows = FIELDS * levs
    outer = cos_out.shape[0]
    used = pl.cdiv(points_dev, INNER)
    slots, _, lanes = incoming.shape
    bands = slots // levs
    band_id = lax.axis_index("band")
    lev_id = lax.axis_index("lev")
    me = band_id * levs + lev_id
    length = length_ref[band_id]
    base = lev_id * points_dev
    inverse_length = 1.0 / jnp.full((1, lanes), length, jnp.int32).astype(jnp.float32)
    factor = inverse_length * weight_ref[band_id]

    barrier = pltpu.get_barrier_semaphore()

    def other(step):
        peer = (me + step) % slots
        return peer // levs, peer % levs

    @pl.loop(1, slots)
    def _(step):
        band, lev = other(step)
        pl.semaphore_signal(
            barrier, inc=1, device_id={"band": band, "lev": lev}, device_id_type=pl.DeviceIdType.MESH
        )

    parts = []
    for i in range(blocks):
        low = low_ref[:, i * pairs : (i + 1) * pairs]
        parts += [low, TRUNC - low]
    if lanes > blocks * each:
        parts.append(jnp.full((bands, lanes - blocks * each), 1 << 14, jnp.int32))
    wave_ref[...] = jnp.concatenate(parts, axis=1)
    mine = jnp.broadcast_to(wave_ref[pl.ds(band_id, 1), :].astype(jnp.float32), (8, lanes)).T
    for i in range(blocks):
        limit_ref[i * pairs : (i + 1) * pairs] = TRUNC + 1 - mine[
            i * each : i * each + pairs, 0:1
        ].astype(jnp.int32)

    def tables(c):
        span = pl.ds(pl.multiple_of(c * lanes, lanes), lanes)
        wave = wave_ref[pl.ds(c, 1), :]
        eight = lax.broadcasted_iota(jnp.int32, (8, lanes), 0)
        c0, s0 = sincos(wave, eight, length, inverse_length)
        c1, s1 = sincos(wave, eight * 8, length, inverse_length)
        c2, s2 = sincos(wave, eight * 64, length, inverse_length)
        steps = lax.broadcasted_iota(jnp.int32, (outer, lanes), 0)
        c3, s3 = sincos(wave, base + steps * INNER, length, inverse_length)
        cos_out[:, span] = c3
        sin_out[:, span] = s3
        for high in range(INNER // 64):
            ch, sh = c2[high : high + 1], s2[high : high + 1]
            for mid in range(8):
                cm, sm = c1[mid : mid + 1], s1[mid : mid + 1]
                cj, sj = ch * cm - sh * sm, ch * sm + sh * cm
                at = high * 64 + mid * 8
                cos_tab[at : at + 8, span] = (c0 * cj - s0 * sj).astype(jnp.bfloat16)
                sin_tab[at : at + 8, span] = (s0 * cj + c0 * sj).astype(jnp.bfloat16)

    early = bands // 2
    pl.loop(0, early)(tables)
    mask = diagonal(pairs, cycles)
    column = lax.broadcasted_iota(jnp.int32, (pairs, packed), 1)

    @pl.loop(0, blocks)
    def _(i):
        part = pl.ds(pl.multiple_of(i * pairs, pairs), pairs)
        lower = column < limit_ref[part]
        read_spec(i).wait()
        halves = []
        for s in range(2):
            for f in range(FIELDS):
                row = spec_vmem[s, f, 0, part].astype(jnp.float32)
                halves += [jnp.where(lower, row, 0.0), jnp.where(lower, 0.0, row)]
        spec = jnp.concatenate(halves, axis=0).astype(jnp.bfloat16)
        read_chunk(leg_hbm, leg_vmem, leg_sem, pairs, i).wait()
        leg = leg_vmem[part].reshape(pairs * cycles, packed)
        full = lax.dot_general(
            leg, spec, (((1,), (1,)), ((), ())), preferred_element_type=jnp.float32
        )
        full = full.reshape(pairs, cycles, 8 * pairs)
        four_ref[i] = jnp.sum(jnp.where(mask, full, 0.0), axis=0)

    sides = []
    for k in range(4):
        parts = [four_ref[i, :, k * each : (k + 1) * each] for i in range(blocks)]
        if lanes > blocks * each:
            parts.append(jnp.zeros((cycles, lanes - blocks * each), jnp.float32))
        sides.append(jnp.concatenate(parts, axis=1))
    for j in range(cycles):
        block = jnp.concatenate([side[j : j + 1] for side in sides], axis=0)
        outgoing[j] = block.astype(jnp.bfloat16)

    pl.semaphore_wait(barrier, slots - 1)

    @pl.loop(1, slots)
    def _(step):
        band, lev = other(step)
        pltpu.make_async_remote_copy(
            src_ref=outgoing.at[band], dst_ref=incoming.at[me], send_sem=send_sem,
            recv_sem=recv_sem, device_id={"band": band, "lev": lev},
            device_id_type=pl.DeviceIdType.MESH,
        ).start()

    incoming[me] = outgoing[band_id]
    pl.loop(early, bands)(tables)

    def wait_all(semaphore, buffer):
        most = buffer.at[pl.ds(0, slots - 1)]
        pltpu.make_async_copy(most, most, semaphore).wait()

    wait_all(recv_sem, incoming)

    @pl.loop(0, bands)
    def _(c):
        span = pl.ds(pl.multiple_of(c * lanes, lanes), lanes)
        wave = wave_ref[pl.ds(c, 1), :]
        gain = jnp.where(wave == 0, 1.0, 2.0)
        live = 2 * wave < length
        cells = [incoming[c * levs + lev].astype(jnp.float32) for lev in range(levs)]
        order = [(f, lev) for f in range(FIELDS) for lev in range(levs)]
        re = jnp.concatenate([cells[lev][f : f + 1] for f, lev in order], axis=0)
        im = jnp.concatenate([cells[lev][FIELDS + f : FIELDS + f + 1] for f, lev in order], axis=0)
        re = jnp.where(live, re * gain, 0.0)
        im = jnp.where(live, im * gain, 0.0)
        for a in range(used):
            co, so = cos_out[a : a + 1, span], sin_out[a : a + 1, span]
            twist_re[a * rows : (a + 1) * rows, span] = (re * co - im * so).astype(jnp.bfloat16)
            twist_im[a * rows : (a + 1) * rows, span] = -(re * so + im * co).astype(jnp.bfloat16)

    contract = (((1,), (1,)), ((), ()))
    grid = lax.dot_general(
        twist_re[...], cos_tab[...], contract, preferred_element_type=jnp.float32
    ) + lax.dot_general(twist_im[...], sin_tab[...], contract, preferred_element_type=jnp.float32)
    lane = lax.broadcasted_iota(jnp.int32, (rows, INNER), 1)
    mixing = mixing_ref[...].astype(jnp.float32)
    updated = []
    for a in range(used):
        point = a * INNER + lane
        inside = (point < points_dev) & (base + point < length)
        cell = jnp.where(inside, grid[a * rows : (a + 1) * rows], 0.0)
        product = (cell[:levs] * cell[levs:]).astype(jnp.bfloat16).astype(jnp.float32)
        total = cell + forcing_ref[:, a * INNER : (a + 1) * INNER].astype(jnp.float32)
        for l2 in range(levs):
            total = total + mixing[:, l2 : l2 + 1] * product[l2 : l2 + 1]
        updated.append(jnp.where(inside, total, 0.0))
    updated = jnp.concatenate(updated, axis=0).astype(jnp.bfloat16)

    def send_band(band):
        @pl.loop(0, levs)
        def _(lev):
            @pl.when((band != band_id) | (lev != lev_id))
            def _():
                pltpu.make_async_remote_copy(
                    src_ref=partial.at[band * levs + lev], dst_ref=arrived.at[me],
                    send_sem=send_back, recv_sem=recv_back, device_id={"band": band, "lev": lev},
                    device_id_type=pl.DeviceIdType.MESH,
                ).start()

    @pl.loop(0, bands)
    def _(c):
        span = pl.ds(pl.multiple_of(c * lanes, lanes), lanes)
        cos_part = jnp.dot(updated, cos_tab[:, span], preferred_element_type=jnp.float32)
        sin_part = jnp.dot(updated, sin_tab[:, span], preferred_element_type=jnp.float32)
        re = jnp.zeros((rows, lanes), jnp.float32)
        im = jnp.zeros((rows, lanes), jnp.float32)
        for a in range(used):
            co, so = cos_out[a : a + 1, span], sin_out[a : a + 1, span]
            cp, sp = cos_part[a * rows : (a + 1) * rows], sin_part[a * rows : (a + 1) * rows]
            re = re + (cp * co - sp * so)
            im = im + (cp * so + sp * co)
        keep = 2 * wave_ref[pl.ds(c, 1), :] < length
        re = jnp.where(keep, re * factor, 0.0)
        im = jnp.where(keep, im * -factor, 0.0)
        for lev in range(levs):
            picks = [side[f * levs + lev : f * levs + lev + 1] for side in (re, im) for f in range(FIELDS)]
            partial[c * levs + lev] = jnp.concatenate(picks, axis=0).astype(jnp.bfloat16)

        @pl.when(c > 0)
        def _():
            send_band(c - 1)

    arrived[me] = partial[me]
    send_band(bands - 1)
    wait_all(recv_back, arrived)
    sums = []
    for j in range(cycles):
        total = arrived[j * levs].astype(jnp.float32)
        for lev in range(1, levs):
            total = total + arrived[j * levs + lev].astype(jnp.float32)
        sums.append(total)
    for k in range(4):
        side = jnp.concatenate([total[k : k + 1] for total in sums], axis=0)
        for i in range(blocks):
            out_ref[i, :, k * each : (k + 1) * each] = side[:, i * each : (i + 1) * each]
    wait_all(send_sem, incoming)
    wait_all(send_back, arrived)


def on_device(spectral, legendre, cycle_len, pair_wave, quad_weight, forcing, mixing):
    band_count = lax.axis_size("band")
    lev_count = lax.axis_size("lev")
    pair_dev = spectral.shape[3]
    cycles = legendre.shape[1]
    levels, points_dev = forcing.shape[1], forcing.shape[3]
    rows = FIELDS * levels
    pairs = pair_block(pair_dev)
    blocks = pair_dev // pairs

    each_band = pl.cdiv(2 * pair_dev, 128) * 128
    waves = band_count * each_band
    used = pl.cdiv(points_dev, INNER)
    outer = pl.cdiv(used, 8) * 8
    force = jnp.pad(forcing.reshape(rows, points_dev), ((0, 0), (0, used * INNER - points_dev)))
    vmem = pl.BlockSpec(memory_space=pltpu.VMEM)
    smem = pl.BlockSpec(memory_space=pltpu.SMEM)
    slots = band_count * lev_count
    message = pltpu.VMEM((slots, 2 * FIELDS, each_band), jnp.bfloat16)
    hbm = pl.BlockSpec(memory_space=pl.ANY)
    coeff, limit = pl.pallas_call(
        functools.partial(grid_kernel, points_dev, lev_count),
        in_specs=[smem, smem, vmem, vmem, vmem, hbm, hbm],
        out_specs=[vmem, vmem],
        out_shape=[
            jax.ShapeDtypeStruct((blocks, cycles, 8 * pairs), jnp.float32),
            jax.ShapeDtypeStruct((pair_dev, 1), jnp.int32),
        ],
        scratch_shapes=[
            pltpu.VMEM((INNER, waves), jnp.bfloat16),
            pltpu.VMEM((INNER, waves), jnp.bfloat16),
            pltpu.VMEM((outer, waves), jnp.float32),
            pltpu.VMEM((outer, waves), jnp.float32),
            pltpu.VMEM((used * rows, waves), jnp.bfloat16),
            pltpu.VMEM((used * rows, waves), jnp.bfloat16),
            pltpu.VMEM((cycles, 2 * FIELDS, each_band), jnp.bfloat16),
            message, message, message,
            pltpu.VMEM(legendre.shape, jnp.bfloat16),
            pltpu.VMEM(spectral.shape, jnp.bfloat16),
            pltpu.VMEM((blocks, cycles, 8 * pairs), jnp.float32),
            pltpu.VMEM((band_count, each_band), jnp.int32),
        ]
        + [pltpu.SemaphoreType.DMA] * 4
        + [pltpu.SemaphoreType.DMA((blocks,))] * 2,
        compiler_params=pltpu.CompilerParams(collective_id=0, has_side_effects=True),
    )(
        cycle_len, quad_weight, pair_wave.reshape(band_count, pair_dev), force,
        mixing.reshape(rows, levels), spectral, legendre,
    )
    return pl.pallas_call(
        direct_kernel,
        in_specs=[vmem, vmem, hbm],
        out_specs=hbm,
        out_shape=jax.ShapeDtypeStruct(spectral.shape, jnp.bfloat16),
        scratch_shapes=[
            pltpu.VMEM(legendre.shape, jnp.bfloat16),
            pltpu.VMEM(spectral.shape, jnp.bfloat16),
        ]
        + [pltpu.SemaphoreType.DMA((blocks,))] * 2,
    )(limit, coeff, legendre)


def solution(mesh):
    return jax.shard_map(
        on_device,
        mesh=mesh,
        in_specs=(
            P(None, None, "lev", "band", None),
            P("band", None, None),
            P(),
            P(),
            P(),
            P(None, None, "band", "lev"),
            P(),
        ),
        out_specs=P(None, None, "lev", "band", None),
        check_vma=False,
    )
```

```python
import functools

import jax
import jax.numpy as jnp
from jax import lax
from jax.experimental import pallas as pl
from jax.experimental.pallas import tpu as pltpu
from jax.sharding import PartitionSpec as P

TRUNC = 2559
FIELDS = 2
INNER = 256
TWO_PI = 6.283185307179586


def pair_block(pair_dev):
    return 16 if pair_dev % 16 == 0 else 8


def sincos(wave, point, length, inverse_length):
    number = wave * point
    turns = jnp.floor(number.astype(jnp.float32) * inverse_length).astype(jnp.int32)
    residue = (number - turns * length).astype(jnp.float32) * inverse_length
    quarter = jnp.floor(residue * 4.0 + 0.5)
    t = (residue - quarter * 0.25) * TWO_PI
    t2 = t * t
    sin_t = t * (1.0 + t2 * (-1.0 / 6 + t2 * (1.0 / 120 + t2 * (-1.0 / 5040 + t2 * (1.0 / 362880)))))
    cos_t = 1.0 + t2 * (
        -0.5 + t2 * (1.0 / 24 + t2 * (-1.0 / 720 + t2 * (1.0 / 40320 + t2 * (-1.0 / 3628800))))
    )
    q = quarter.astype(jnp.int32)
    swap = (q & 1) == 1
    cos_v = jnp.where(swap, sin_t, cos_t)
    sin_v = jnp.where(swap, cos_t, sin_t)
    cos_v = jnp.where(((q + 1) & 2) == 2, -cos_v, cos_v)
    sin_v = jnp.where((q & 2) == 2, -sin_v, sin_v)
    return cos_v, sin_v


def diagonal(pairs, cycles):
    rows = lax.broadcasted_iota(jnp.int32, (pairs, cycles, 8 * pairs), 0)
    lanes = lax.broadcasted_iota(jnp.int32, (pairs, cycles, 8 * pairs), 2) % pairs
    return rows == lanes


def read_chunk(leg_hbm, leg_vmem, sem, pairs, i):
    part = pl.ds(pl.multiple_of(i * pairs, pairs), pairs)
    return pltpu.make_async_copy(leg_hbm.at[part], leg_vmem.at[part], sem.at[i])


def direct_kernel(split, limit_ref, coeff_ref, leg_hbm, out_hbm, leg_vmem, out_vmem, in_sem, out_sem):
    blocks, cycles, wide_lanes = coeff_ref.shape
    pairs = wide_lanes // 8
    packed = leg_vmem.shape[2]

    def write(i):
        part = pl.ds(pl.multiple_of(i * pairs, pairs), pairs)
        return pltpu.make_async_copy(
            out_vmem.at[:, :, :, part], out_hbm.at[:, :, :, part], out_sem.at[i]
        )

    for i in range(blocks):
        read_chunk(leg_hbm, leg_vmem, in_sem, pairs, i).start()
    mask = diagonal(pairs, cycles)
    column = split + lax.broadcasted_iota(jnp.int32, (pairs, packed - split), 1)
    half = 4 * pairs

    @pl.loop(0, blocks)
    def _(i):
        part = pl.ds(pl.multiple_of(i * pairs, pairs), pairs)
        wide = jnp.broadcast_to(coeff_ref[pl.ds(i, 1)], (pairs, cycles, 8 * pairs))
        wide = jnp.where(mask, wide, 0.0).reshape(pairs * cycles, 8 * pairs)
        wide = wide.T.astype(jnp.bfloat16)
        lower = column < limit_ref[part]
        read_chunk(leg_hbm, leg_vmem, in_sem, pairs, i).wait()
        leg = leg_vmem[part].reshape(pairs * cycles, packed)
        left = jnp.dot(wide[:half], leg[:, :split], preferred_element_type=jnp.float32)
        right = jnp.dot(wide, leg[:, split:], preferred_element_type=jnp.float32)
        for s in range(2):
            for f in range(FIELDS):
                at = (s * FIELDS + f) * pairs
                out_vmem[s, f, 0, part, :split] = left[at : at + pairs].astype(jnp.bfloat16)
                low, high = right[at : at + pairs], right[half + at : half + at + pairs]
                out_vmem[s, f, 0, part, split:] = jnp.where(lower, low, high).astype(jnp.bfloat16)
        write(i).start()

    for i in range(blocks):
        write(i).wait()


def grid_kernel(
    points_dev, levs, split, length_ref, weight_ref, low_ref, forcing_ref, mixing_ref, spec_hbm, leg_hbm,
    out_ref, limit_ref,
    cos_tab, sin_tab, cos_out, sin_out, twist_re, twist_im,
    outgoing, incoming, partial, arrived, leg_vmem, spec_vmem, four_ref, wave_ref,
    send_sem, recv_sem, send_back, recv_back, leg_sem, spec_sem,
):
    blocks, cycles, wide = four_ref.shape
    pairs = wide // 8
    packed = leg_vmem.shape[2]
    each = wide // 4

    def read_spec(i):
        part = pl.ds(pl.multiple_of(i * pairs, pairs), pairs)
        return pltpu.make_async_copy(
            spec_hbm.at[:, :, :, part], spec_vmem.at[:, :, :, part], spec_sem.at[i]
        )

    for i in range(blocks):
        read_spec(i).start()
        read_chunk(leg_hbm, leg_vmem, leg_sem, pairs, i).start()
    rows = FIELDS * levs
    outer = cos_out.shape[0]
    used = pl.cdiv(points_dev, INNER)
    slots, _, lanes = incoming.shape
    bands = slots // levs
    band_id = lax.axis_index("band")
    lev_id = lax.axis_index("lev")
    me = band_id * levs + lev_id
    length = length_ref[band_id]
    base = lev_id * points_dev
    inverse_length = 1.0 / jnp.full((1, lanes), length, jnp.int32).astype(jnp.float32)
    factor = inverse_length * weight_ref[band_id]

    barrier = pltpu.get_barrier_semaphore()

    def other(step):
        peer = (me + step) % slots
        return peer // levs, peer % levs

    @pl.loop(1, slots)
    def _(step):
        band, lev = other(step)
        pl.semaphore_signal(
            barrier, inc=1, device_id={"band": band, "lev": lev}, device_id_type=pl.DeviceIdType.MESH
        )

    parts = [low_ref[...], TRUNC - low_ref[...]]
    if lanes > blocks * each:
        parts.append(jnp.full((bands, lanes - blocks * each), 1 << 14, jnp.int32))
    wave_ref[...] = jnp.concatenate(parts, axis=1)
    mine = jnp.broadcast_to(wave_ref[pl.ds(band_id, 1), :].astype(jnp.float32), (8, lanes)).T
    limit_ref[...] = TRUNC + 1 - mine[: blocks * pairs, 0:1].astype(jnp.int32)

    def tables(c):
        span = pl.ds(pl.multiple_of(c * lanes, lanes), lanes)
        wave = wave_ref[pl.ds(c, 1), :]
        eight = lax.broadcasted_iota(jnp.int32, (8, lanes), 0)
        c0, s0 = sincos(wave, eight, length, inverse_length)
        c1, s1 = sincos(wave, eight * 8, length, inverse_length)
        c2, s2 = sincos(wave, eight * 64, length, inverse_length)
        steps = lax.broadcasted_iota(jnp.int32, (outer, lanes), 0)
        c3, s3 = sincos(wave, base + steps * INNER, length, inverse_length)
        cos_out[:, span] = c3
        sin_out[:, span] = s3
        for high in range(INNER // 64):
            ch, sh = c2[high : high + 1], s2[high : high + 1]
            for mid in range(8):
                cm, sm = c1[mid : mid + 1], s1[mid : mid + 1]
                cj, sj = ch * cm - sh * sm, ch * sm + sh * cm
                at = high * 64 + mid * 8
                cos_tab[at : at + 8, span] = (c0 * cj - s0 * sj).astype(jnp.bfloat16)
                sin_tab[at : at + 8, span] = (s0 * cj + c0 * sj).astype(jnp.bfloat16)

    early = bands // 2
    pl.loop(0, early)(tables)
    mask = diagonal(pairs, cycles)
    column = split + lax.broadcasted_iota(jnp.int32, (pairs, packed - split), 1)
    inner = (((1,), (1,)), ((), ()))

    @pl.loop(0, blocks)
    def _(i):
        part = pl.ds(pl.multiple_of(i * pairs, pairs), pairs)
        lower = column < limit_ref[part]
        read_spec(i).wait()
        whole, lows, highs = [], [], []
        for s in range(2):
            for f in range(FIELDS):
                whole.append(spec_vmem[s, f, 0, part, :split])
                row = spec_vmem[s, f, 0, part, split:].astype(jnp.float32)
                lows.append(jnp.where(lower, row, 0.0))
                highs.append(jnp.where(lower, 0.0, row))
        left = jnp.concatenate(whole, axis=0)
        right = jnp.concatenate(lows + highs, axis=0).astype(jnp.bfloat16)
        read_chunk(leg_hbm, leg_vmem, leg_sem, pairs, i).wait()
        leg = leg_vmem[part].reshape(pairs * cycles, packed)
        full = lax.dot_general(leg[:, split:], right, inner, preferred_element_type=jnp.float32)
        some = lax.dot_general(leg[:, :split], left, inner, preferred_element_type=jnp.float32)
        full = full + jnp.concatenate([some, jnp.zeros_like(some)], axis=1)
        full = full.reshape(pairs, cycles, 8 * pairs)
        four_ref[i] = jnp.sum(jnp.where(mask, full, 0.0), axis=0)

    sides = []
    for k in range(4):
        parts = [
            four_ref[i, :, (4 * h + k) * pairs : (4 * h + k + 1) * pairs]
            for h in range(2)
            for i in range(blocks)
        ]
        if lanes > blocks * each:
            parts.append(jnp.zeros((cycles, lanes - blocks * each), jnp.float32))
        sides.append(jnp.concatenate(parts, axis=1))
    for j in range(cycles):
        block = jnp.concatenate([side[j : j + 1] for side in sides], axis=0)
        outgoing[j] = block.astype(jnp.bfloat16)

    pl.semaphore_wait(barrier, slots - 1)

    @pl.loop(1, slots)
    def _(step):
        band, lev = other(step)
        pltpu.make_async_remote_copy(
            src_ref=outgoing.at[band], dst_ref=incoming.at[me], send_sem=send_sem,
            recv_sem=recv_sem, device_id={"band": band, "lev": lev},
            device_id_type=pl.DeviceIdType.MESH,
        ).start()

    incoming[me] = outgoing[band_id]
    pl.loop(early, bands)(tables)

    def wait_all(semaphore, buffer):
        most = buffer.at[pl.ds(0, slots - 1)]
        pltpu.make_async_copy(most, most, semaphore).wait()

    wait_all(recv_sem, incoming)

    @pl.loop(0, bands)
    def _(c):
        span = pl.ds(pl.multiple_of(c * lanes, lanes), lanes)
        wave = wave_ref[pl.ds(c, 1), :]
        gain = jnp.where(wave == 0, 1.0, 2.0)
        live = 2 * wave < length
        cells = [incoming[c * levs + lev].astype(jnp.float32) for lev in range(levs)]
        order = [(f, lev) for f in range(FIELDS) for lev in range(levs)]
        re = jnp.concatenate([cells[lev][f : f + 1] for f, lev in order], axis=0)
        im = jnp.concatenate([cells[lev][FIELDS + f : FIELDS + f + 1] for f, lev in order], axis=0)
        re = jnp.where(live, re * gain, 0.0)
        im = jnp.where(live, im * gain, 0.0)
        for a in range(used):
            co, so = cos_out[a : a + 1, span], sin_out[a : a + 1, span]
            twist_re[a * rows : (a + 1) * rows, span] = (re * co - im * so).astype(jnp.bfloat16)
            twist_im[a * rows : (a + 1) * rows, span] = -(re * so + im * co).astype(jnp.bfloat16)

    contract = (((1,), (1,)), ((), ()))
    grid = lax.dot_general(
        twist_re[...], cos_tab[...], contract, preferred_element_type=jnp.float32
    ) + lax.dot_general(twist_im[...], sin_tab[...], contract, preferred_element_type=jnp.float32)
    lane = lax.broadcasted_iota(jnp.int32, (rows, INNER), 1)
    mixing = mixing_ref[...].astype(jnp.float32)
    updated = []
    for a in range(used):
        point = a * INNER + lane
        inside = (point < points_dev) & (base + point < length)
        cell = jnp.where(inside, grid[a * rows : (a + 1) * rows], 0.0)
        product = (cell[:levs] * cell[levs:]).astype(jnp.bfloat16).astype(jnp.float32)
        total = cell + forcing_ref[:, a * INNER : (a + 1) * INNER].astype(jnp.float32)
        for l2 in range(levs):
            total = total + mixing[:, l2 : l2 + 1] * product[l2 : l2 + 1]
        updated.append(jnp.where(inside, total, 0.0))
    updated = jnp.concatenate(updated, axis=0).astype(jnp.bfloat16)

    def send_band(band):
        @pl.loop(0, levs)
        def _(lev):
            @pl.when((band != band_id) | (lev != lev_id))
            def _():
                pltpu.make_async_remote_copy(
                    src_ref=partial.at[band * levs + lev], dst_ref=arrived.at[me],
                    send_sem=send_back, recv_sem=recv_back, device_id={"band": band, "lev": lev},
                    device_id_type=pl.DeviceIdType.MESH,
                ).start()

    @pl.loop(0, bands)
    def _(c):
        span = pl.ds(pl.multiple_of(c * lanes, lanes), lanes)
        cos_part = jnp.dot(updated, cos_tab[:, span], preferred_element_type=jnp.float32)
        sin_part = jnp.dot(updated, sin_tab[:, span], preferred_element_type=jnp.float32)
        re = jnp.zeros((rows, lanes), jnp.float32)
        im = jnp.zeros((rows, lanes), jnp.float32)
        for a in range(used):
            co, so = cos_out[a : a + 1, span], sin_out[a : a + 1, span]
            cp, sp = cos_part[a * rows : (a + 1) * rows], sin_part[a * rows : (a + 1) * rows]
            re = re + (cp * co - sp * so)
            im = im + (cp * so + sp * co)
        keep = 2 * wave_ref[pl.ds(c, 1), :] < length
        re = jnp.where(keep, re * factor, 0.0)
        im = jnp.where(keep, im * -factor, 0.0)
        for lev in range(levs):
            picks = [side[f * levs + lev : f * levs + lev + 1] for side in (re, im) for f in range(FIELDS)]
            partial[c * levs + lev] = jnp.concatenate(picks, axis=0).astype(jnp.bfloat16)

        @pl.when(c > 0)
        def _():
            send_band(c - 1)

    arrived[me] = partial[me]
    send_band(bands - 1)
    wait_all(recv_back, arrived)
    sums = []
    for j in range(cycles):
        total = arrived[j * levs].astype(jnp.float32)
        for lev in range(1, levs):
            total = total + arrived[j * levs + lev].astype(jnp.float32)
        sums.append(total)
    for k in range(4):
        side = jnp.concatenate([total[k : k + 1] for total in sums], axis=0)
        for h in range(2):
            for i in range(blocks):
                at, lane = (4 * h + k) * pairs, (h * blocks + i) * pairs
                out_ref[i, :, at : at + pairs] = side[:, lane : lane + pairs]
    wait_all(send_sem, incoming)
    wait_all(send_back, arrived)


def on_device(spectral, legendre, cycle_len, pair_wave, quad_weight, forcing, mixing):
    band_count = lax.axis_size("band")
    lev_count = lax.axis_size("lev")
    pair_dev = spectral.shape[3]
    cycles = legendre.shape[1]
    levels, points_dev = forcing.shape[1], forcing.shape[3]
    rows = FIELDS * levels
    pairs = pair_block(pair_dev)
    blocks = pair_dev // pairs

    each_band = pl.cdiv(2 * pair_dev, 128) * 128
    waves = band_count * each_band
    used = pl.cdiv(points_dev, INNER)
    outer = pl.cdiv(used, 8) * 8
    force = jnp.pad(forcing.reshape(rows, points_dev), ((0, 0), (0, used * INNER - points_dev)))
    vmem = pl.BlockSpec(memory_space=pltpu.VMEM)
    smem = pl.BlockSpec(memory_space=pltpu.SMEM)
    slots = band_count * lev_count
    message = pltpu.VMEM((slots, 2 * FIELDS, each_band), jnp.bfloat16)
    split = (TRUNC + 2 - pair_wave.shape[0]) // 128 * 128
    hbm = pl.BlockSpec(memory_space=pl.ANY)
    coeff, limit = pl.pallas_call(
        functools.partial(grid_kernel, points_dev, lev_count, split),
        in_specs=[smem, smem, vmem, vmem, vmem, hbm, hbm],
        out_specs=[vmem, vmem],
        out_shape=[
            jax.ShapeDtypeStruct((blocks, cycles, 8 * pairs), jnp.float32),
            jax.ShapeDtypeStruct((pair_dev, 1), jnp.int32),
        ],
        scratch_shapes=[
            pltpu.VMEM((INNER, waves), jnp.bfloat16),
            pltpu.VMEM((INNER, waves), jnp.bfloat16),
            pltpu.VMEM((outer, waves), jnp.float32),
            pltpu.VMEM((outer, waves), jnp.float32),
            pltpu.VMEM((used * rows, waves), jnp.bfloat16),
            pltpu.VMEM((used * rows, waves), jnp.bfloat16),
            pltpu.VMEM((cycles, 2 * FIELDS, each_band), jnp.bfloat16),
            message, message, message,
            pltpu.VMEM(legendre.shape, jnp.bfloat16),
            pltpu.VMEM(spectral.shape, jnp.bfloat16),
            pltpu.VMEM((blocks, cycles, 8 * pairs), jnp.float32),
            pltpu.VMEM((band_count, each_band), jnp.int32),
        ]
        + [pltpu.SemaphoreType.DMA] * 4
        + [pltpu.SemaphoreType.DMA((blocks,))] * 2,
        compiler_params=pltpu.CompilerParams(collective_id=0, has_side_effects=True),
    )(
        cycle_len, quad_weight, pair_wave.reshape(band_count, pair_dev), force,
        mixing.reshape(rows, levels), spectral, legendre,
    )
    return pl.pallas_call(
        functools.partial(direct_kernel, split),
        in_specs=[vmem, vmem, hbm],
        out_specs=hbm,
        out_shape=jax.ShapeDtypeStruct(spectral.shape, jnp.bfloat16),
        scratch_shapes=[
            pltpu.VMEM(legendre.shape, jnp.bfloat16),
            pltpu.VMEM(spectral.shape, jnp.bfloat16),
        ]
        + [pltpu.SemaphoreType.DMA((blocks,))] * 2,
    )(limit, coeff, legendre)


def solution(mesh):
    return jax.shard_map(
        on_device,
        mesh=mesh,
        in_specs=(
            P(None, None, "lev", "band", None),
            P("band", None, None),
            P(),
            P(),
            P(),
            P(None, None, "band", "lev"),
            P(),
        ),
        out_specs=P(None, None, "lev", "band", None),
        check_vma=False,
    )
```

```python
import functools

import jax
import jax.numpy as jnp
from jax import lax
from jax.experimental import pallas as pl
from jax.experimental.pallas import tpu as pltpu
from jax.sharding import PartitionSpec as P

TRUNC = 2559
FIELDS = 2
INNER = 256
TWO_PI = 6.283185307179586


def pair_block(pair_dev):
    return 16 if pair_dev % 16 == 0 else 8


def sincos(wave, point, length, inverse_length):
    number = wave * point
    turns = jnp.floor(number.astype(jnp.float32) * inverse_length).astype(jnp.int32)
    residue = (number - turns * length).astype(jnp.float32) * inverse_length
    quarter = jnp.floor(residue * 4.0 + 0.5)
    t = (residue - quarter * 0.25) * TWO_PI
    t2 = t * t
    sin_t = t * (1.0 + t2 * (-1.0 / 6 + t2 * (1.0 / 120 + t2 * (-1.0 / 5040 + t2 * (1.0 / 362880)))))
    cos_t = 1.0 + t2 * (
        -0.5 + t2 * (1.0 / 24 + t2 * (-1.0 / 720 + t2 * (1.0 / 40320 + t2 * (-1.0 / 3628800))))
    )
    q = quarter.astype(jnp.int32)
    swap = (q & 1) == 1
    cos_v = jnp.where(swap, sin_t, cos_t)
    sin_v = jnp.where(swap, cos_t, sin_t)
    cos_v = jnp.where(((q + 1) & 2) == 2, -cos_v, cos_v)
    sin_v = jnp.where((q & 2) == 2, -sin_v, sin_v)
    return cos_v, sin_v


def diagonal(pairs, cycles):
    rows = lax.broadcasted_iota(jnp.int32, (pairs, cycles, 8 * pairs), 0)
    lanes = lax.broadcasted_iota(jnp.int32, (pairs, cycles, 8 * pairs), 2) % pairs
    return rows == lanes


def read_chunk(leg_hbm, leg_vmem, sem, pairs, i):
    part = pl.ds(pl.multiple_of(i * pairs, pairs), pairs)
    return pltpu.make_async_copy(leg_hbm.at[part], leg_vmem.at[part], sem.at[i])


def direct_kernel(split, limit_ref, coeff_ref, leg_hbm, out_hbm, leg_vmem, out_vmem, in_sem, out_sem):
    blocks, cycles, wide_lanes = coeff_ref.shape
    pairs = wide_lanes // 8
    packed = leg_vmem.shape[2]

    def write(i):
        part = pl.ds(pl.multiple_of(i * pairs, pairs), pairs)
        return pltpu.make_async_copy(
            out_vmem.at[:, :, :, part], out_hbm.at[:, :, :, part], out_sem.at[i]
        )

    for i in range(blocks):
        read_chunk(leg_hbm, leg_vmem, in_sem, pairs, i).start()
    mask = diagonal(pairs, cycles)
    column = split + lax.broadcasted_iota(jnp.int32, (pairs, packed - split), 1)
    half = 4 * pairs

    @pl.loop(0, blocks)
    def _(i):
        part = pl.ds(pl.multiple_of(i * pairs, pairs), pairs)
        wide = jnp.broadcast_to(coeff_ref[pl.ds(i, 1)], (pairs, cycles, 8 * pairs))
        wide = jnp.where(mask, wide, 0.0).reshape(pairs * cycles, 8 * pairs)
        wide = wide.T.astype(jnp.bfloat16)
        lower = column < limit_ref[part]
        read_chunk(leg_hbm, leg_vmem, in_sem, pairs, i).wait()
        leg = leg_vmem[part].reshape(pairs * cycles, packed)
        left = jnp.dot(wide[:half], leg[:, :split], preferred_element_type=jnp.float32)
        right = jnp.dot(wide, leg[:, split:], preferred_element_type=jnp.float32)
        for s in range(2):
            for f in range(FIELDS):
                at = (s * FIELDS + f) * pairs
                out_vmem[s, f, 0, part, :split] = left[at : at + pairs].astype(jnp.bfloat16)
                low, high = right[at : at + pairs], right[half + at : half + at + pairs]
                out_vmem[s, f, 0, part, split:] = jnp.where(lower, low, high).astype(jnp.bfloat16)
        write(i).start()

    for i in range(blocks):
        write(i).wait()


def grid_kernel(
    points_dev, levs, split, length_ref, weight_ref, low_ref, forcing_ref, mixing_ref, spec_hbm, leg_hbm,
    out_ref, limit_ref,
    cos_tab, sin_tab, cos_out, sin_out, twist_re, twist_im,
    outgoing, incoming, partial, arrived, leg_vmem, spec_vmem, four_ref, wave_ref,
    send_sem, recv_sem, send_back, recv_back, leg_sem, spec_sem,
):
    blocks, cycles, wide = four_ref.shape
    pairs = wide // 8
    packed = leg_vmem.shape[2]
    each = wide // 4

    def read_spec(i):
        part = pl.ds(pl.multiple_of(i * pairs, pairs), pairs)
        return pltpu.make_async_copy(
            spec_hbm.at[:, :, :, part], spec_vmem.at[:, :, :, part], spec_sem.at[i]
        )

    for i in range(blocks):
        read_spec(i).start()
        read_chunk(leg_hbm, leg_vmem, leg_sem, pairs, i).start()
    rows = FIELDS * levs
    outer = cos_out.shape[0]
    used = pl.cdiv(points_dev, INNER)
    slots, _, lanes = incoming.shape
    bands = slots // levs
    band_id = lax.axis_index("band")
    lev_id = lax.axis_index("lev")
    me = band_id * levs + lev_id
    length = length_ref[band_id]
    base = lev_id * points_dev
    inverse_length = 1.0 / jnp.full((1, lanes), length, jnp.int32).astype(jnp.float32)
    factor = inverse_length * weight_ref[band_id]

    barrier = pltpu.get_barrier_semaphore()

    def other(step):
        peer = (me + step) % slots
        return peer // levs, peer % levs

    @pl.loop(1, slots)
    def _(step):
        band, lev = other(step)
        pl.semaphore_signal(
            barrier, inc=1, device_id={"band": band, "lev": lev}, device_id_type=pl.DeviceIdType.MESH
        )

    own = blocks * pairs
    low = jnp.concatenate([low_ref[:, k * own : (k + 1) * own] for k in range(bands)], axis=0)
    parts = [low, TRUNC - low]
    if lanes > blocks * each:
        parts.append(jnp.full((bands, lanes - blocks * each), 1 << 14, jnp.int32))
    wave_ref[...] = jnp.concatenate(parts, axis=1)
    mine = jnp.broadcast_to(wave_ref[pl.ds(band_id, 1), :].astype(jnp.float32), (8, lanes)).T
    limit_ref[...] = TRUNC + 1 - mine[: blocks * pairs, 0:1].astype(jnp.int32)

    def tables(c):
        span = pl.ds(pl.multiple_of(c * lanes, lanes), lanes)
        wave = wave_ref[pl.ds(c, 1), :]
        eight = lax.broadcasted_iota(jnp.int32, (8, lanes), 0)
        c0, s0 = sincos(wave, eight, length, inverse_length)
        c1, s1 = sincos(wave, eight * 8, length, inverse_length)
        c2, s2 = sincos(wave, eight * 64, length, inverse_length)
        steps = lax.broadcasted_iota(jnp.int32, (outer, lanes), 0)
        c3, s3 = sincos(wave, base + steps * INNER, length, inverse_length)
        cos_out[:, span] = c3
        sin_out[:, span] = s3
        for high in range(INNER // 64):
            ch, sh = c2[high : high + 1], s2[high : high + 1]
            for mid in range(8):
                cm, sm = c1[mid : mid + 1], s1[mid : mid + 1]
                cj, sj = ch * cm - sh * sm, ch * sm + sh * cm
                at = high * 64 + mid * 8
                cos_tab[at : at + 8, span] = (c0 * cj - s0 * sj).astype(jnp.bfloat16)
                sin_tab[at : at + 8, span] = (s0 * cj + c0 * sj).astype(jnp.bfloat16)

    early = bands // 2
    pl.loop(0, early)(tables)
    mask = diagonal(pairs, cycles)
    column = split + lax.broadcasted_iota(jnp.int32, (pairs, packed - split), 1)
    inner = (((1,), (1,)), ((), ()))

    @pl.loop(0, blocks)
    def _(i):
        part = pl.ds(pl.multiple_of(i * pairs, pairs), pairs)
        lower = column < limit_ref[part]
        read_spec(i).wait()
        whole, lows, highs = [], [], []
        for s in range(2):
            for f in range(FIELDS):
                whole.append(spec_vmem[s, f, 0, part, :split])
                row = spec_vmem[s, f, 0, part, split:].astype(jnp.float32)
                lows.append(jnp.where(lower, row, 0.0))
                highs.append(jnp.where(lower, 0.0, row))
        left = jnp.concatenate(whole, axis=0)
        right = jnp.concatenate(lows + highs, axis=0).astype(jnp.bfloat16)
        read_chunk(leg_hbm, leg_vmem, leg_sem, pairs, i).wait()
        leg = leg_vmem[part].reshape(pairs * cycles, packed)
        full = lax.dot_general(leg[:, split:], right, inner, preferred_element_type=jnp.float32)
        some = lax.dot_general(leg[:, :split], left, inner, preferred_element_type=jnp.float32)
        full = full + jnp.concatenate([some, jnp.zeros_like(some)], axis=1)
        full = full.reshape(pairs, cycles, 8 * pairs)
        four_ref[i] = jnp.sum(jnp.where(mask, full, 0.0), axis=0)

    sides = []
    for k in range(4):
        parts = [
            four_ref[i, :, (4 * h + k) * pairs : (4 * h + k + 1) * pairs]
            for h in range(2)
            for i in range(blocks)
        ]
        if lanes > blocks * each:
            parts.append(jnp.zeros((cycles, lanes - blocks * each), jnp.float32))
        sides.append(jnp.concatenate(parts, axis=1))
    for j in range(cycles):
        block = jnp.concatenate([side[j : j + 1] for side in sides], axis=0)
        outgoing[j] = block.astype(jnp.bfloat16)

    pl.semaphore_wait(barrier, slots - 1)

    @pl.loop(1, slots)
    def _(step):
        band, lev = other(step)
        pltpu.make_async_remote_copy(
            src_ref=outgoing.at[band], dst_ref=incoming.at[me], send_sem=send_sem,
            recv_sem=recv_sem, device_id={"band": band, "lev": lev},
            device_id_type=pl.DeviceIdType.MESH,
        ).start()

    incoming[me] = outgoing[band_id]
    pl.loop(early, bands)(tables)

    def wait_all(semaphore, buffer):
        most = buffer.at[pl.ds(0, slots - 1)]
        pltpu.make_async_copy(most, most, semaphore).wait()

    wait_all(recv_sem, incoming)

    @pl.loop(0, bands)
    def _(c):
        span = pl.ds(pl.multiple_of(c * lanes, lanes), lanes)
        wave = wave_ref[pl.ds(c, 1), :]
        gain = jnp.where(wave == 0, 1.0, 2.0)
        live = 2 * wave < length
        cells = [incoming[c * levs + lev].astype(jnp.float32) for lev in range(levs)]
        order = [(f, lev) for f in range(FIELDS) for lev in range(levs)]
        re = jnp.concatenate([cells[lev][f : f + 1] for f, lev in order], axis=0)
        im = jnp.concatenate([cells[lev][FIELDS + f : FIELDS + f + 1] for f, lev in order], axis=0)
        re = jnp.where(live, re * gain, 0.0)
        im = jnp.where(live, im * gain, 0.0)
        for a in range(used):
            co, so = cos_out[a : a + 1, span], sin_out[a : a + 1, span]
            twist_re[a * rows : (a + 1) * rows, span] = (re * co - im * so).astype(jnp.bfloat16)
            twist_im[a * rows : (a + 1) * rows, span] = -(re * so + im * co).astype(jnp.bfloat16)

    contract = (((1,), (1,)), ((), ()))
    grid = lax.dot_general(
        twist_re[...], cos_tab[...], contract, preferred_element_type=jnp.float32
    ) + lax.dot_general(twist_im[...], sin_tab[...], contract, preferred_element_type=jnp.float32)
    lane = lax.broadcasted_iota(jnp.int32, (rows, INNER), 1)
    mixing = mixing_ref[...].astype(jnp.float32)
    updated = []
    for a in range(used):
        point = a * INNER + lane
        inside = (point < points_dev) & (base + point < length)
        cell = jnp.where(inside, grid[a * rows : (a + 1) * rows], 0.0)
        product = (cell[:levs] * cell[levs:]).astype(jnp.bfloat16).astype(jnp.float32)
        total = cell + forcing_ref[:, a * INNER : (a + 1) * INNER].astype(jnp.float32)
        for l2 in range(levs):
            total = total + mixing[:, l2 : l2 + 1] * product[l2 : l2 + 1]
        updated.append(jnp.where(inside, total, 0.0))
    updated = jnp.concatenate(updated, axis=0).astype(jnp.bfloat16)

    def send_band(band):
        @pl.loop(1, levs + 1)
        def _(turn):
            lev = (lev_id + turn) % levs

            @pl.when((band != band_id) | (lev != lev_id))
            def _():
                pltpu.make_async_remote_copy(
                    src_ref=partial.at[band * levs + lev], dst_ref=arrived.at[me],
                    send_sem=send_back, recv_sem=recv_back, device_id={"band": band, "lev": lev},
                    device_id_type=pl.DeviceIdType.MESH,
                ).start()

    @pl.loop(0, bands)
    def _(turn):
        c = (band_id + 1 + turn) % bands
        span = pl.ds(pl.multiple_of(c * lanes, lanes), lanes)
        cos_part = jnp.dot(updated, cos_tab[:, span], preferred_element_type=jnp.float32)
        sin_part = jnp.dot(updated, sin_tab[:, span], preferred_element_type=jnp.float32)
        re = jnp.zeros((rows, lanes), jnp.float32)
        im = jnp.zeros((rows, lanes), jnp.float32)
        for a in range(used):
            co, so = cos_out[a : a + 1, span], sin_out[a : a + 1, span]
            cp, sp = cos_part[a * rows : (a + 1) * rows], sin_part[a * rows : (a + 1) * rows]
            re = re + (cp * co - sp * so)
            im = im + (cp * so + sp * co)
        keep = 2 * wave_ref[pl.ds(c, 1), :] < length
        re = jnp.where(keep, re * factor, 0.0)
        im = jnp.where(keep, im * -factor, 0.0)
        for lev in range(levs):
            picks = [side[f * levs + lev : f * levs + lev + 1] for side in (re, im) for f in range(FIELDS)]
            partial[c * levs + lev] = jnp.concatenate(picks, axis=0).astype(jnp.bfloat16)

        @pl.when(turn > 0)
        def _():
            send_band((band_id + turn) % bands)

    arrived[me] = partial[me]
    send_band(band_id)
    wait_all(recv_back, arrived)
    sums = []
    for j in range(cycles):
        total = arrived[j * levs].astype(jnp.float32)
        for lev in range(1, levs):
            total = total + arrived[j * levs + lev].astype(jnp.float32)
        sums.append(total)
    for k in range(4):
        side = jnp.concatenate([total[k : k + 1] for total in sums], axis=0)
        for h in range(2):
            for i in range(blocks):
                at, lane = (4 * h + k) * pairs, (h * blocks + i) * pairs
                out_ref[i, :, at : at + pairs] = side[:, lane : lane + pairs]
    wait_all(send_sem, incoming)
    wait_all(send_back, arrived)


def on_device(spectral, legendre, cycle_len, pair_wave, quad_weight, forcing, mixing):
    band_count = lax.axis_size("band")
    lev_count = lax.axis_size("lev")
    pair_dev = spectral.shape[3]
    cycles = legendre.shape[1]
    levels, points_dev = forcing.shape[1], forcing.shape[3]
    rows = FIELDS * levels
    pairs = pair_block(pair_dev)
    blocks = pair_dev // pairs

    each_band = pl.cdiv(2 * pair_dev, 128) * 128
    waves = band_count * each_band
    used = pl.cdiv(points_dev, INNER)
    outer = pl.cdiv(used, 8) * 8
    force = jnp.pad(forcing.reshape(rows, points_dev), ((0, 0), (0, used * INNER - points_dev)))
    vmem = pl.BlockSpec(memory_space=pltpu.VMEM)
    smem = pl.BlockSpec(memory_space=pltpu.SMEM)
    slots = band_count * lev_count
    message = pltpu.VMEM((slots, 2 * FIELDS, each_band), jnp.bfloat16)
    split = (TRUNC + 2 - pair_wave.shape[0]) // 128 * 128
    hbm = pl.BlockSpec(memory_space=pl.ANY)
    coeff, limit = pl.pallas_call(
        functools.partial(grid_kernel, points_dev, lev_count, split),
        in_specs=[smem, smem, vmem, vmem, vmem, hbm, hbm],
        out_specs=[vmem, vmem],
        out_shape=[
            jax.ShapeDtypeStruct((blocks, cycles, 8 * pairs), jnp.float32),
            jax.ShapeDtypeStruct((pair_dev, 1), jnp.int32),
        ],
        scratch_shapes=[
            pltpu.VMEM((INNER, waves), jnp.bfloat16),
            pltpu.VMEM((INNER, waves), jnp.bfloat16),
            pltpu.VMEM((outer, waves), jnp.float32),
            pltpu.VMEM((outer, waves), jnp.float32),
            pltpu.VMEM((used * rows, waves), jnp.bfloat16),
            pltpu.VMEM((used * rows, waves), jnp.bfloat16),
            pltpu.VMEM((cycles, 2 * FIELDS, each_band), jnp.bfloat16),
            message, message, message,
            pltpu.VMEM(legendre.shape, jnp.bfloat16),
            pltpu.VMEM(spectral.shape, jnp.bfloat16),
            pltpu.VMEM((blocks, cycles, 8 * pairs), jnp.float32),
            pltpu.VMEM((band_count, each_band), jnp.int32),
        ]
        + [pltpu.SemaphoreType.DMA] * 4
        + [pltpu.SemaphoreType.DMA((blocks,))] * 2,
        compiler_params=pltpu.CompilerParams(collective_id=0, has_side_effects=True),
    )(
        cycle_len, quad_weight, pair_wave.reshape(1, -1), force,
        mixing.reshape(rows, levels), spectral, legendre,
    )
    return pl.pallas_call(
        functools.partial(direct_kernel, split),
        in_specs=[vmem, vmem, hbm],
        out_specs=hbm,
        out_shape=jax.ShapeDtypeStruct(spectral.shape, jnp.bfloat16),
        scratch_shapes=[
            pltpu.VMEM(legendre.shape, jnp.bfloat16),
            pltpu.VMEM(spectral.shape, jnp.bfloat16),
        ]
        + [pltpu.SemaphoreType.DMA((blocks,))] * 2,
    )(limit, coeff, legendre)


def solution(mesh):
    return jax.shard_map(
        on_device,
        mesh=mesh,
        in_specs=(
            P(None, None, "lev", "band", None),
            P("band", None, None),
            P(),
            P(),
            P(),
            P(None, None, "band", "lev"),
            P(),
        ),
        out_specs=P(None, None, "lev", "band", None),
        check_vma=False,
    )
```

```python
import functools

import jax
import jax.numpy as jnp
from jax import lax
from jax.experimental import pallas as pl
from jax.experimental.pallas import tpu as pltpu
from jax.sharding import PartitionSpec as P

TRUNC = 2559
FIELDS = 2
INNER = 256
TWO_PI = 6.283185307179586


def pair_block(pair_dev):
    return 16 if pair_dev % 16 == 0 else 8


def sincos(wave, point, length, inverse_length):
    number = wave * point
    turns = jnp.floor(number.astype(jnp.float32) * inverse_length).astype(jnp.int32)
    residue = (number - turns * length).astype(jnp.float32) * inverse_length
    quarter = jnp.floor(residue * 4.0 + 0.5)
    t = (residue - quarter * 0.25) * TWO_PI
    t2 = t * t
    sin_t = t * (1.0 + t2 * (-1.0 / 6 + t2 * (1.0 / 120 + t2 * (-1.0 / 5040 + t2 * (1.0 / 362880)))))
    cos_t = 1.0 + t2 * (
        -0.5 + t2 * (1.0 / 24 + t2 * (-1.0 / 720 + t2 * (1.0 / 40320 + t2 * (-1.0 / 3628800))))
    )
    q = quarter.astype(jnp.int32)
    swap = (q & 1) == 1
    cos_v = jnp.where(swap, sin_t, cos_t)
    sin_v = jnp.where(swap, cos_t, sin_t)
    cos_v = jnp.where(((q + 1) & 2) == 2, -cos_v, cos_v)
    sin_v = jnp.where((q & 2) == 2, -sin_v, sin_v)
    return cos_v, sin_v


def diagonal(pairs, cycles):
    rows = lax.broadcasted_iota(jnp.int32, (pairs, cycles, 8 * pairs), 0)
    lanes = lax.broadcasted_iota(jnp.int32, (pairs, cycles, 8 * pairs), 2) % pairs
    return rows == lanes


def read_chunk(leg_hbm, leg_vmem, sem, pairs, i):
    part = pl.ds(pl.multiple_of(i * pairs, pairs), pairs)
    return pltpu.make_async_copy(leg_hbm.at[part], leg_vmem.at[part], sem.at[i])


def direct_kernel(split, limit_ref, coeff_ref, leg_hbm, out_hbm, leg_vmem, out_vmem, in_sem, out_sem):
    blocks, cycles, wide_lanes = coeff_ref.shape
    pairs = wide_lanes // 8
    packed = leg_vmem.shape[2]

    def write(i):
        part = pl.ds(pl.multiple_of(i * pairs, pairs), pairs)
        return pltpu.make_async_copy(
            out_vmem.at[:, :, :, part], out_hbm.at[:, :, :, part], out_sem.at[i]
        )

    for i in range(blocks):
        read_chunk(leg_hbm, leg_vmem, in_sem, pairs, i).start()
    mask = diagonal(pairs, cycles)
    column = split + lax.broadcasted_iota(jnp.int32, (pairs, packed - split), 1)
    half = 4 * pairs

    @pl.loop(0, blocks)
    def _(i):
        part = pl.ds(pl.multiple_of(i * pairs, pairs), pairs)
        wide = jnp.broadcast_to(coeff_ref[pl.ds(i, 1)], (pairs, cycles, 8 * pairs))
        wide = jnp.where(mask, wide, 0.0).reshape(pairs * cycles, 8 * pairs)
        wide = wide.T.astype(jnp.bfloat16)
        lower = column < limit_ref[part]
        read_chunk(leg_hbm, leg_vmem, in_sem, pairs, i).wait()
        leg = leg_vmem[part].reshape(pairs * cycles, packed)
        left = jnp.dot(wide[:half], leg[:, :split], preferred_element_type=jnp.float32)
        right = jnp.dot(wide, leg[:, split:], preferred_element_type=jnp.float32)
        for s in range(2):
            for f in range(FIELDS):
                at = (s * FIELDS + f) * pairs
                out_vmem[s, f, 0, part, :split] = left[at : at + pairs].astype(jnp.bfloat16)
                low, high = right[at : at + pairs], right[half + at : half + at + pairs]
                out_vmem[s, f, 0, part, split:] = jnp.where(lower, low, high).astype(jnp.bfloat16)
        write(i).start()

    for i in range(blocks):
        write(i).wait()


def grid_kernel(
    points_dev, levs, split, length_ref, weight_ref, low_ref, forcing_ref, mixing_ref, spec_hbm, leg_hbm,
    out_ref, limit_ref,
    cos_tab, sin_tab, cos_out, sin_out, twist_re, twist_im,
    outgoing, incoming, partial, arrived, leg_vmem, spec_vmem, four_ref, wave_ref,
    send_sem, recv_sem, send_back, recv_back, leg_sem, spec_sem,
):
    blocks, cycles, wide = four_ref.shape
    pairs = wide // 8
    packed = leg_vmem.shape[2]
    each = wide // 4

    def read_spec(i):
        part = pl.ds(pl.multiple_of(i * pairs, pairs), pairs)
        return pltpu.make_async_copy(
            spec_hbm.at[:, :, :, part], spec_vmem.at[:, :, :, part], spec_sem.at[i]
        )

    for i in range(blocks):
        read_spec(i).start()
        read_chunk(leg_hbm, leg_vmem, leg_sem, pairs, i).start()
    rows = FIELDS * levs
    outer = cos_out.shape[0]
    used = pl.cdiv(points_dev, INNER)
    slots, _, lanes = incoming.shape
    bands = slots // levs
    band_id = lax.axis_index("band")
    lev_id = lax.axis_index("lev")
    me = band_id * levs + lev_id
    length = length_ref[band_id]
    base = lev_id * points_dev
    inverse_length = 1.0 / jnp.full((1, lanes), length, jnp.int32).astype(jnp.float32)
    factor = inverse_length * weight_ref[band_id]

    barrier = pltpu.get_barrier_semaphore()

    def other(step):
        peer = (me + step) % slots
        return peer // levs, peer % levs

    @pl.loop(1, slots)
    def _(step):
        band, lev = other(step)
        pl.semaphore_signal(
            barrier, inc=1, device_id={"band": band, "lev": lev}, device_id_type=pl.DeviceIdType.MESH
        )

    own = blocks * pairs
    line = low_ref[...].reshape(1, bands * own)
    low = jnp.concatenate([line[:, k * own : (k + 1) * own] for k in range(bands)], axis=0)
    parts = [low, TRUNC - low]
    if lanes > blocks * each:
        parts.append(jnp.full((bands, lanes - blocks * each), 1 << 14, jnp.int32))
    wave_ref[...] = jnp.concatenate(parts, axis=1)
    mine = jnp.broadcast_to(wave_ref[pl.ds(band_id, 1), :].astype(jnp.float32), (8, lanes)).T
    limit_ref[...] = TRUNC + 1 - mine[: blocks * pairs, 0:1].astype(jnp.int32)

    def tables(c):
        span = pl.ds(pl.multiple_of(c * lanes, lanes), lanes)
        wave = wave_ref[pl.ds(c, 1), :]
        eight = lax.broadcasted_iota(jnp.int32, (8, lanes), 0)
        c0, s0 = sincos(wave, eight, length, inverse_length)
        c1, s1 = sincos(wave, eight * 8, length, inverse_length)
        c2, s2 = sincos(wave, eight * 64, length, inverse_length)
        steps = lax.broadcasted_iota(jnp.int32, (outer, lanes), 0)
        c3, s3 = sincos(wave, base + steps * INNER, length, inverse_length)
        cos_out[:, span] = c3
        sin_out[:, span] = s3
        for high in range(INNER // 64):
            ch, sh = c2[high : high + 1], s2[high : high + 1]
            for mid in range(8):
                cm, sm = c1[mid : mid + 1], s1[mid : mid + 1]
                cj, sj = ch * cm - sh * sm, ch * sm + sh * cm
                at = high * 64 + mid * 8
                cos_tab[at : at + 8, span] = (c0 * cj - s0 * sj).astype(jnp.bfloat16)
                sin_tab[at : at + 8, span] = (s0 * cj + c0 * sj).astype(jnp.bfloat16)

    early = bands // 2
    pl.loop(0, early)(tables)
    mask = diagonal(pairs, cycles)
    column = split + lax.broadcasted_iota(jnp.int32, (pairs, packed - split), 1)
    inner = (((1,), (1,)), ((), ()))

    @pl.loop(0, blocks)
    def _(i):
        part = pl.ds(pl.multiple_of(i * pairs, pairs), pairs)
        lower = column < limit_ref[part]
        read_spec(i).wait()
        whole, lows, highs = [], [], []
        for s in range(2):
            for f in range(FIELDS):
                whole.append(spec_vmem[s, f, 0, part, :split])
                row = spec_vmem[s, f, 0, part, split:].astype(jnp.float32)
                lows.append(jnp.where(lower, row, 0.0))
                highs.append(jnp.where(lower, 0.0, row))
        left = jnp.concatenate(whole, axis=0)
        right = jnp.concatenate(lows + highs, axis=0).astype(jnp.bfloat16)
        read_chunk(leg_hbm, leg_vmem, leg_sem, pairs, i).wait()
        leg = leg_vmem[part].reshape(pairs * cycles, packed)
        full = lax.dot_general(leg[:, split:], right, inner, preferred_element_type=jnp.float32)
        some = lax.dot_general(leg[:, :split], left, inner, preferred_element_type=jnp.float32)
        full = full + jnp.concatenate([some, jnp.zeros_like(some)], axis=1)
        full = full.reshape(pairs, cycles, 8 * pairs)
        four_ref[i] = jnp.sum(jnp.where(mask, full, 0.0), axis=0)

    sides = []
    for k in range(4):
        parts = [
            four_ref[i, :, (4 * h + k) * pairs : (4 * h + k + 1) * pairs]
            for h in range(2)
            for i in range(blocks)
        ]
        if lanes > blocks * each:
            parts.append(jnp.zeros((cycles, lanes - blocks * each), jnp.float32))
        sides.append(jnp.concatenate(parts, axis=1))
    for j in range(cycles):
        block = jnp.concatenate([side[j : j + 1] for side in sides], axis=0)
        outgoing[j] = block.astype(jnp.bfloat16)

    pl.semaphore_wait(barrier, slots - 1)

    @pl.loop(1, slots)
    def _(step):
        band, lev = other(step)
        pltpu.make_async_remote_copy(
            src_ref=outgoing.at[band], dst_ref=incoming.at[me], send_sem=send_sem,
            recv_sem=recv_sem, device_id={"band": band, "lev": lev},
            device_id_type=pl.DeviceIdType.MESH,
        ).start()

    incoming[me] = outgoing[band_id]
    pl.loop(early, bands)(tables)

    def wait_all(semaphore, buffer):
        most = buffer.at[pl.ds(0, slots - 1)]
        pltpu.make_async_copy(most, most, semaphore).wait()

    wait_all(recv_sem, incoming)

    @pl.loop(0, bands)
    def _(c):
        span = pl.ds(pl.multiple_of(c * lanes, lanes), lanes)
        wave = wave_ref[pl.ds(c, 1), :]
        gain = jnp.where(wave == 0, 1.0, 2.0)
        live = 2 * wave < length
        cells = [incoming[c * levs + lev].astype(jnp.float32) for lev in range(levs)]
        order = [(f, lev) for f in range(FIELDS) for lev in range(levs)]
        re = jnp.concatenate([cells[lev][f : f + 1] for f, lev in order], axis=0)
        im = jnp.concatenate([cells[lev][FIELDS + f : FIELDS + f + 1] for f, lev in order], axis=0)
        re = jnp.where(live, re * gain, 0.0)
        im = jnp.where(live, im * gain, 0.0)
        for a in range(used):
            co, so = cos_out[a : a + 1, span], sin_out[a : a + 1, span]
            twist_re[a * rows : (a + 1) * rows, span] = (re * co - im * so).astype(jnp.bfloat16)
            twist_im[a * rows : (a + 1) * rows, span] = -(re * so + im * co).astype(jnp.bfloat16)

    contract = (((1,), (1,)), ((), ()))
    grid = lax.dot_general(
        twist_re[...], cos_tab[...], contract, preferred_element_type=jnp.float32
    ) + lax.dot_general(twist_im[...], sin_tab[...], contract, preferred_element_type=jnp.float32)
    lane = lax.broadcasted_iota(jnp.int32, (rows, INNER), 1)
    mixing = mixing_ref[...].astype(jnp.float32)
    updated = []
    for a in range(used):
        point = a * INNER + lane
        inside = (point < points_dev) & (base + point < length)
        cell = jnp.where(inside, grid[a * rows : (a + 1) * rows], 0.0)
        product = (cell[:levs] * cell[levs:]).astype(jnp.bfloat16).astype(jnp.float32)
        force = forcing_ref[:, a * INNER : min((a + 1) * INNER, points_dev)].astype(jnp.float32)
        if force.shape[1] < INNER:
            rest = jnp.zeros((rows, INNER - force.shape[1]), jnp.float32)
            force = jnp.concatenate([force, rest], axis=1)
        total = cell + force
        for l2 in range(levs):
            total = total + mixing[:, l2 : l2 + 1] * product[l2 : l2 + 1]
        updated.append(jnp.where(inside, total, 0.0))
    updated = jnp.concatenate(updated, axis=0).astype(jnp.bfloat16)

    def send_band(band):
        @pl.loop(0, levs)
        def _(lev):
            @pl.when((band != band_id) | (lev != lev_id))
            def _():
                pltpu.make_async_remote_copy(
                    src_ref=partial.at[band * levs + lev], dst_ref=arrived.at[me],
                    send_sem=send_back, recv_sem=recv_back, device_id={"band": band, "lev": lev},
                    device_id_type=pl.DeviceIdType.MESH,
                ).start()

    @pl.loop(0, bands)
    def _(c):
        span = pl.ds(pl.multiple_of(c * lanes, lanes), lanes)
        cos_part = jnp.dot(updated, cos_tab[:, span], preferred_element_type=jnp.float32)
        sin_part = jnp.dot(updated, sin_tab[:, span], preferred_element_type=jnp.float32)
        re = jnp.zeros((rows, lanes), jnp.float32)
        im = jnp.zeros((rows, lanes), jnp.float32)
        for a in range(used):
            co, so = cos_out[a : a + 1, span], sin_out[a : a + 1, span]
            cp, sp = cos_part[a * rows : (a + 1) * rows], sin_part[a * rows : (a + 1) * rows]
            re = re + (cp * co - sp * so)
            im = im + (cp * so + sp * co)
        keep = 2 * wave_ref[pl.ds(c, 1), :] < length
        re = jnp.where(keep, re * factor, 0.0)
        im = jnp.where(keep, im * -factor, 0.0)
        for lev in range(levs):
            picks = [side[f * levs + lev : f * levs + lev + 1] for side in (re, im) for f in range(FIELDS)]
            partial[c * levs + lev] = jnp.concatenate(picks, axis=0).astype(jnp.bfloat16)

        @pl.when(c > 0)
        def _():
            send_band(c - 1)

    arrived[me] = partial[me]
    send_band(bands - 1)
    wait_all(recv_back, arrived)
    sums = []
    for j in range(cycles):
        total = arrived[j * levs].astype(jnp.float32)
        for lev in range(1, levs):
            total = total + arrived[j * levs + lev].astype(jnp.float32)
        sums.append(total)
    for k in range(4):
        side = jnp.concatenate([total[k : k + 1] for total in sums], axis=0)
        for h in range(2):
            for i in range(blocks):
                at, lane = (4 * h + k) * pairs, (h * blocks + i) * pairs
                out_ref[i, :, at : at + pairs] = side[:, lane : lane + pairs]
    wait_all(send_sem, incoming)
    wait_all(send_back, arrived)


def on_device(spectral, legendre, cycle_len, pair_wave, quad_weight, forcing, mixing):
    band_count = lax.axis_size("band")
    lev_count = lax.axis_size("lev")
    pair_dev = spectral.shape[3]
    cycles = legendre.shape[1]
    levels, points_dev = forcing.shape[1], forcing.shape[3]
    rows = FIELDS * levels
    pairs = pair_block(pair_dev)
    blocks = pair_dev // pairs

    each_band = pl.cdiv(2 * pair_dev, 128) * 128
    waves = band_count * each_band
    used = pl.cdiv(points_dev, INNER)
    outer = pl.cdiv(used, 8) * 8
    force = forcing.reshape(rows, points_dev)
    vmem = pl.BlockSpec(memory_space=pltpu.VMEM)
    smem = pl.BlockSpec(memory_space=pltpu.SMEM)
    slots = band_count * lev_count
    message = pltpu.VMEM((slots, 2 * FIELDS, each_band), jnp.bfloat16)
    split = (TRUNC + 2 - pair_wave.shape[0]) // 128 * 128
    hbm = pl.BlockSpec(memory_space=pl.ANY)
    coeff, limit = pl.pallas_call(
        functools.partial(grid_kernel, points_dev, lev_count, split),
        in_specs=[smem, smem, vmem, vmem, vmem, hbm, hbm],
        out_specs=[vmem, vmem],
        out_shape=[
            jax.ShapeDtypeStruct((blocks, cycles, 8 * pairs), jnp.float32),
            jax.ShapeDtypeStruct((pair_dev, 1), jnp.int32),
        ],
        scratch_shapes=[
            pltpu.VMEM((INNER, waves), jnp.bfloat16),
            pltpu.VMEM((INNER, waves), jnp.bfloat16),
            pltpu.VMEM((outer, waves), jnp.float32),
            pltpu.VMEM((outer, waves), jnp.float32),
            pltpu.VMEM((used * rows, waves), jnp.bfloat16),
            pltpu.VMEM((used * rows, waves), jnp.bfloat16),
            pltpu.VMEM((cycles, 2 * FIELDS, each_band), jnp.bfloat16),
            message, message, message,
            pltpu.VMEM(legendre.shape, jnp.bfloat16),
            pltpu.VMEM(spectral.shape, jnp.bfloat16),
            pltpu.VMEM((blocks, cycles, 8 * pairs), jnp.float32),
            pltpu.VMEM((band_count, each_band), jnp.int32),
        ]
        + [pltpu.SemaphoreType.DMA] * 4
        + [pltpu.SemaphoreType.DMA((blocks,))] * 2,
        compiler_params=pltpu.CompilerParams(collective_id=0, has_side_effects=True),
    )(
        cycle_len, quad_weight, pair_wave, force,
        mixing.reshape(rows, levels), spectral, legendre,
    )
    return pl.pallas_call(
        functools.partial(direct_kernel, split),
        in_specs=[vmem, vmem, hbm],
        out_specs=hbm,
        out_shape=jax.ShapeDtypeStruct(spectral.shape, jnp.bfloat16),
        scratch_shapes=[
            pltpu.VMEM(legendre.shape, jnp.bfloat16),
            pltpu.VMEM(spectral.shape, jnp.bfloat16),
        ]
        + [pltpu.SemaphoreType.DMA((blocks,))] * 2,
    )(limit, coeff, legendre)


def solution(mesh):
    return jax.shard_map(
        on_device,
        mesh=mesh,
        in_specs=(
            P(None, None, "lev", "band", None),
            P("band", None, None),
            P(),
            P(),
            P(),
            P(None, None, "band", "lev"),
            P(),
        ),
        out_specs=P(None, None, "lev", "band", None),
        check_vma=False,
    )
```
